128 devices in a mesh: row: 8 (over z, core), col: 16 (over x, y).
Axes of the slice: x: 4, y: 4, z: 4, core: 2. Of those that a mesh axis runs over, the one named last changes fastest.
Arguments:
- rate_terms: bfloat16 [6, 8192, 8192], P(None, 'row', 'col'), may hold values from -1 to 1
- populations: float32 [8192, 256], P(('row', 'col')), may hold values from 0.05 to 1
- temp_bins: int32 [256], replicated, may hold values from 0 to 63
- bin_coeffs: float32 [64, 6], replicated, may hold values from -1 to 1
Outputs:
- updated: float32 [8192, 256], P(('row', 'col'))
The draws below stay inside these ranges and needn't reach their ends.
All inputs are finite; a program needn't handle non-finite values.
Results may differ from the reference program's by a relative error of at most 0.0011.
Values may be sent and summed in bfloat16 or wider, within the bound.
No kernel may reach another device: no remote copies, remote signals or barrier semaphores. Data moves between devices by JAX's collectives and lax.ppermute only.
A program may use at most 64 MiB of HBM per device.

```python
import math
import jax
import jax.numpy as jnp
from jax import lax

LEVELS = 8192
CELLS = 256
TERMS = 6
NBINS = 64
KRYLOV = 4
TAYLOR = 8


mode_count = 6


rough_scale = 0.8


def draw_rate_terms(key, part):
    position = (jnp.arange(LEVELS, dtype=jnp.float32) + 0.5) * (math.pi / LEVELS)
    smooth_modes = []
    for order in range(mode_count):
        factor = math.sqrt(1.0 / LEVELS) if order == 0 else math.sqrt(2.0 / LEVELS)
        smooth_modes.append(factor * jnp.cos(order * position))
    matrices = []
    for number in range(TERMS):
        term_key = jax.random.fold_in(key, 101 + number)
        rough_key = jax.random.fold_in(term_key, 7)
        coupling_key = jax.random.fold_in(term_key, 11)
        rough_part = jnp.clip(jax.random.normal(rough_key, (LEVELS, LEVELS), jnp.float32), -6.0, 6.0)
        coupling = 0.7 * jnp.clip(jax.random.normal(coupling_key, (mode_count, mode_count), jnp.float32), -3.0, 3.0)
        matrix = rough_scale / math.sqrt(LEVELS) * rough_part
        for target in range(mode_count):
            column_mode = coupling[0, target] * smooth_modes[0]
            for order in range(1, mode_count):
                column_mode = column_mode + coupling[order, target] * smooth_modes[order]
            matrix = matrix + column_mode[:, None] * smooth_modes[target][None, :]
        matrices.append(matrix.astype(jnp.bfloat16))
    return jnp.stack(matrices)


def plant(values, own_key, low, largest):
    spot = [jax.random.randint(jax.random.fold_in(own_key, axis), (), 0, length) for axis, length in enumerate(values.shape)]
    main_axis = values.shape.index(max(values.shape))
    beside = spot[:main_axis] + [(spot[main_axis] + 1) % values.shape[main_axis]] + spot[main_axis + 1:]
    return values.at[tuple(spot)].set(low).at[tuple(beside)].set(largest)


def block_scale(rng, extent, shards, least, high):
    loudness, own = 1.0, jax.random.fold_in(rng, 6)
    for axis_at, shards_of in shards:
        draws = jnp.exp(jax.random.uniform(jax.random.fold_in(own, axis_at), (shards_of,), jnp.float32, least / len(shards), high / len(shards)))
        loudness = loudness * jnp.repeat(draws, extent[axis_at] // shards_of).reshape([-1 if axis == axis_at else 1 for axis in range(len(extent))])
    return loudness


def setup_inputs(seed: int = 0) -> dict:
    splits = jax.random.split(jax.random.key(seed), 5)
    rate_terms = draw_rate_terms(jax.random.fold_in(splits[4], 71), 0)
    populations = jnp.clip(jnp.exp(math.log(1.0) - 2.9957323 * jax.random.uniform(splits[1], (LEVELS, CELLS), jnp.float32) ** block_scale(splits[1], (LEVELS, CELLS), ((0, 128),), -0.2, 0.2)), 0.05, 1.0)
    temp_bins = plant(jax.random.randint(splits[2], (CELLS,), 0, NBINS), jax.random.fold_in(splits[2], 1), 0, NBINS - 1).astype(jnp.int32)
    bin_coeffs = jnp.clip(jax.random.uniform(splits[3], (NBINS, TERMS), jnp.float32, -1.0, 1.0), -1.0, 1.0)
    return dict(rate_terms=rate_terms, populations=populations, temp_bins=temp_bins, bin_coeffs=bin_coeffs)


epsilon = 1e-06
step_size = 1.0

def apply_rates(rate_terms, weights, vector):
    rounded = vector.astype(jnp.bfloat16)
    total = jnp.zeros(vector.shape, jnp.float32)
    for j in range(TERMS):
        product = jnp.dot(rate_terms[j], rounded, preferred_element_type=jnp.float32)
        total = total + weights[:, j][None, :] * product
    return total

def reference(rate_terms, populations, temp_bins, bin_coeffs):
    weights = bin_coeffs[temp_bins.astype(jnp.int32)]
    force = apply_rates(rate_terms, weights, populations)
    scale_norm = jnp.sqrt(lax.optimization_barrier(jnp.sum(force * force, axis=0)) + epsilon)
    basis = [force / scale_norm[None, :]]
    zero_row = jnp.zeros((populations.shape[1],), jnp.float32)
    hessen = [[zero_row for j in range(KRYLOV)] for i in range(KRYLOV)]
    for j in range(KRYLOV):
        fresh = apply_rates(rate_terms, weights, basis[j])
        correlations = [lax.optimization_barrier(jnp.sum(basis[i] * fresh, axis=0)) for i in range(j + 1)]
        for i in range(j + 1):
            fresh = fresh - correlations[i][None, :] * basis[i]
            hessen[i][j] = correlations[i]
        if j < KRYLOV - 1:
            length = jnp.sqrt(lax.optimization_barrier(jnp.sum(fresh * fresh, axis=0)) + epsilon)
            hessen[j + 1][j] = length
            basis.append(fresh / length[None, :])
    hmat = jnp.stack([jnp.stack(line) for line in hessen]) * step_size
    first_unit = jnp.zeros((KRYLOV, populations.shape[1]), jnp.float32).at[0].set(1.0)
    coeffs = first_unit / float(math.factorial(TAYLOR + 1))
    for k in range(TAYLOR - 1, -1, -1):
        coeffs = lax.optimization_barrier(jnp.sum(hmat * coeffs[None, :, :], axis=1)) + first_unit / float(math.factorial(k + 1))
    update = jnp.zeros(populations.shape, jnp.float32)
    for i in range(KRYLOV):
        update = update + coeffs[i][None, :] * basis[i]
    return populations + step_size * scale_norm[None, :] * update
```

```python
import math

import jax
import jax.numpy as jnp
from jax import lax
from jax.experimental import pallas as pl
from jax.experimental.pallas import tpu as pltpu
from jax.sharding import Mesh, PartitionSpec as P

KRYLOV = 4
TAYLOR = 8
TERMS = 6

epsilon = 1e-06
step_size = 1.0

NZ, NK, NX, NY = 4, 2, 4, 4
ALL = ("z", "k", "x", "y")
SUB = 64
HALF = NX * SUB
COLS = NK * HALF
EXTRA = 8


def device(z, k, x, y):
    return ((z * NK + k) * NX + x) * NY + y


TO_INNER = [
    (device(z, k, x, y), device(z, x % 2, y, 2 * k + x // 2))
    for z in range(NZ)
    for k in range(NK)
    for x in range(NX)
    for y in range(NY)
]
TO_OUTER = [(b, a) for a, b in TO_INNER]
SWAP = [(0, 1), (1, 0)]


def solve(gram, count):
    g = lambda m, n: gram[(min(m, n), max(m, n))]
    scale = jnp.sqrt(g(1, 1) + epsilon)
    combos = {1: {1: 1.0 / scale}}
    hess = {(1, 0): scale}
    for j in range(1, count):
        d = {j + 1: None}
        for m in range(1, j + 1):
            d[m] = 0.0
        for i in range(1, j + 1):
            h = 0.0
            for m, c in combos[i].items():
                h = h + c * g(m, j + 1)
            hess[(i, j)] = h
            for m, c in combos[i].items():
                d[m] = d[m] - h * c
        square = g(j + 1, j + 1)
        for m in range(1, j + 1):
            inner = 2.0 * g(m, j + 1)
            for n in range(1, j + 1):
                inner = inner + d[n] * g(m, n)
            square = square + d[m] * inner
        length = jnp.sqrt(jnp.maximum(square, 0.0) + epsilon)
        hess[(j + 1, j)] = length
        inv = 1.0 / length
        combos[j + 1] = {m: (inv if m == j + 1 else d[m] * inv) for m in d}
    return combos, hess


def matmul_kernel(n_fields, exact, k_ref, kept_ref, got_ref, w_ref, *refs):
    own_refs, other_refs = refs[:n_fields], refs[n_fields : 2 * n_fields]
    out_ref, x_ref = refs[2 * n_fields :][:2]
    step = pl.program_id(0)
    core = k_ref[0]
    cells = w_ref.shape[1]

    if not exact:
        gram_ref = refs[2 * n_fields + 2]

    @pl.when(step == 0)
    def _():
        for ref, at in ((own_refs[-1], core * HALF), (other_refs[-1], (1 - core) * HALF)):
            for x in range(NX):
                rows = pl.ds(pl.multiple_of(at + x * SUB, SUB), SUB)
                x_ref[rows, pl.ds(0, cells)] = ref[x, pl.ds(0, SUB), :]
                if not exact:
                    x_ref[rows, pl.ds(cells, cells)] = ref[x, pl.ds(SUB, SUB), :]
        if not exact:
            gram_ref[...] = jnp.zeros_like(gram_ref)
            for m in range(n_fields):
                total = jnp.zeros((8, cells), jnp.float32)
                for a_ref, b_ref in ((own_refs[m], own_refs[-1]), (other_refs[m], other_refs[-1])):
                    for x in range(NX):
                        wide = lambda r: (
                            r[x, pl.ds(0, SUB), :].astype(jnp.float32)
                            + r[x, pl.ds(SUB, SUB), :].astype(jnp.float32)
                        )
                        product = wide(a_ref) * wide(b_ref)
                        total = total + jnp.sum(product.reshape(SUB // 8, 8, cells), axis=0)
                gram_ref[pl.ds(m, 1), :] = jnp.sum(total, axis=0, keepdims=True)

    def part(rates):
        total = None
        for j in range(TERMS):
            product = jnp.dot(rates[j, 0], x_ref[...], preferred_element_type=jnp.float32)
            if not exact:
                product = product[:, :cells] + product[:, cells:]
            product = w_ref[pl.ds(j, 1), :] * product
            total = product if total is None else total + product
        for x in range(NX):
            out_ref[x, 0, pl.ds(0, SUB), :] = total[x * SUB : (x + 1) * SUB, :]
            if not exact:
                out_ref[x, 0, pl.ds(SUB, EXTRA), :] = gram_ref[...]

    @pl.when(step < 2)
    def _():
        part(kept_ref)

    @pl.when(step >= 2)
    def _():
        part(got_ref)


def apply_rates(core, kept, got, weights, fields, exact):
    cells = weights.shape[1]
    rows = SUB if exact else SUB + EXTRA
    whole = lambda a: pl.BlockSpec(a.shape, lambda g, k: (0,) * a.ndim)
    own, other = [f[0] for f in fields], [f[1] for f in fields]
    block = (TERMS, 1, HALF, COLS)
    scratch = [pltpu.VMEM((COLS, cells if exact else 2 * cells), jnp.bfloat16)]
    if not exact:
        scratch.append(pltpu.VMEM((EXTRA, cells), jnp.float32))

    def kernel(*refs):
        matmul_kernel(len(fields), exact, *refs)

    out = pl.pallas_call(
        kernel,
        out_shape=jax.ShapeDtypeStruct((NX, NY, rows, cells), jnp.float32),
        grid_spec=pltpu.PrefetchScalarGridSpec(
            num_scalar_prefetch=1,
            grid=(NY,),
            in_specs=[
                pl.BlockSpec(block, lambda g, k: (0, 2 * jnp.minimum(g, 1) + k[0], 0, 0)),
                pl.BlockSpec(block, lambda g, k: (0, jnp.maximum(g - 2, 0), 0, 0)),
                whole(weights),
                *[whole(a) for a in own],
                *[whole(a) for a in other],
            ],
            out_specs=pl.BlockSpec(
                (NX, 1, rows, cells), lambda g, k: (0, (g + 2 * k[0]) % NY, 0, 0)
            ),
            scratch_shapes=scratch,
        ),
        name="rates",
    )(core, kept, got, weights, *own, *other)
    return out.reshape(NX * NY, rows, cells)


def combine_kernel(j, got_ref, gram_ref, *refs):
    q_refs, outs = refs[:j], refs[j:]
    cells = got_ref.shape[2]
    total = got_ref[0]
    for b in range(1, NX * NY):
        total = total + got_ref[b]
    fresh = total[:SUB]
    gram_out = outs[-1]
    gram = {}
    if j > 0:
        gram_out[...] = gram_ref[...]
        for m in range(1, j + 1):
            for n in range(m, j):
                gram[(m, n)] = gram_ref[pl.ds(4 * (m - 1) + n - 1, 1), :]
            row = total[SUB + m - 1 : SUB + m]
            gram[(m, j)] = row
            gram_out[pl.ds(4 * (m - 1) + j - 1, 1), :] = row
        _, hess = solve(gram, j)
        for i in range(1, j):
            fresh = fresh - hess[(i, j - 1)] * q_refs[i][...]
        fresh = fresh * (1.0 / hess[(j, j - 1)])
    else:
        gram_out[...] = jnp.zeros_like(gram_out)
    if j < KRYLOV:
        q_out, send_out = outs[0], outs[1]
        q_out[...] = fresh
        high = fresh.astype(jnp.bfloat16)
        low = (fresh - high.astype(jnp.float32)).astype(jnp.bfloat16)
        for b in range(NZ * NX):
            send_out[b, pl.ds(0, SUB), :] = high
            send_out[b, pl.ds(SUB, SUB), :] = low
    else:
        dots = outs[0]
        lanes = dots.shape[1]
        for m in range(1, KRYLOV + 1):
            row = jnp.sum(q_refs[m - 1][...] * fresh, axis=0, keepdims=True)
            dots[pl.ds(m - 1, 1), :] = row[:, :lanes]
            dots[pl.ds(KRYLOV + m - 1, 1), :] = row[:, lanes:]


def combine(j, got, gram, fields):
    cells = got.shape[2]

    def kernel(*refs):
        combine_kernel(j, *refs)

    if j < KRYLOV:
        outs = (
            jax.ShapeDtypeStruct((SUB, cells), jnp.float32),
            jax.ShapeDtypeStruct((NZ * NX, 2 * SUB, cells), jnp.bfloat16),
        )
    else:
        outs = (jax.ShapeDtypeStruct((2 * KRYLOV, cells // 2), jnp.float32),)
    return pl.pallas_call(
        kernel,
        out_shape=(*outs, jax.ShapeDtypeStruct(gram.shape, jnp.float32)),
        name=f"combine{j}",
    )(got, gram, *fields)


def finish_kernel(p_ref, q_ref, gram_ref, dots_ref, out_ref):
    gram = {}
    for m in range(1, KRYLOV + 1):
        for n in range(m, KRYLOV + 1):
            gram[(m, n)] = gram_ref[pl.ds(4 * (m - 1) + n - 1, 1), :]
    dots = jnp.sum(dots_ref[...], axis=0)
    last = {
        m: jnp.concatenate([dots[m - 1 : m], dots[KRYLOV + m - 1 : KRYLOV + m]], axis=1)
        for m in range(1, KRYLOV + 1)
    }
    combos, hess = solve(gram, KRYLOV)
    for i in range(1, KRYLOV + 1):
        h = 0.0
        for m, c in combos[i].items():
            h = h + c * last[m]
        hess[(i, KRYLOV)] = h
    zero = jnp.zeros_like(gram[(1, 1)])
    unit = [zero + 1.0] + [zero] * (KRYLOV - 1)
    coeffs = [u / float(math.factorial(TAYLOR + 1)) for u in unit]
    for k in range(TAYLOR - 1, -1, -1):
        fresh = []
        for i in range(1, KRYLOV + 1):
            value = unit[i - 1] / float(math.factorial(k + 1))
            for j in range(max(i - 1, 1), KRYLOV + 1):
                value = value + step_size * hess[(i, j)] * coeffs[j - 1]
            fresh.append(value)
        coeffs = fresh
    out = p_ref[...]
    for m in range(1, KRYLOV + 1):
        factor = 0.0
        for i in range(m, KRYLOV + 1):
            factor = factor + coeffs[i - 1] * combos[i][m]
        out = out + step_size * hess[(1, 0)] * factor * q_ref[m - 1]
    out_ref[...] = out


def body(rate_terms, populations, temp_bins, bin_coeffs):
    core = lax.axis_index("k")
    n_bins = bin_coeffs.shape[0]
    cells = populations.shape[1]
    exchange = lambda v, axes: lax.all_to_all(v, axes, 0, 0, tiled=True)

    rates = rate_terms.reshape(TERMS, 2 * NK, HALF, COLS)
    away = lax.dynamic_index_in_dim(
        rate_terms.reshape(TERMS, 2, NK, HALF, COLS), 1 - core, 2, keepdims=False
    )
    got_rates = lax.ppermute(away, "k", SWAP)

    onehot = (temp_bins[:, None] == jnp.arange(n_bins, dtype=jnp.int32)[None, :]).astype(
        jnp.float32
    )
    weights = jnp.dot(onehot, bin_coeffs, precision=lax.Precision.HIGHEST)
    weights = jnp.pad(weights.T, ((0, 2), (0, 0)))
    core_id = core.astype(jnp.int32).reshape(1)

    def spread(blocks):
        met = exchange(blocks, ("z", "x"))
        own = lax.dynamic_slice_in_dim(met, lax.axis_index("x") * NX, NX, 0)
        return own, lax.ppermute(own, "k", SWAP)

    piece = lax.ppermute(populations.astype(jnp.bfloat16), ALL, TO_INNER)
    field = spread(jnp.broadcast_to(piece[None], (NZ * NX, SUB, cells)))
    met = exchange(apply_rates(core_id, rates, got_rates, weights, [field], True), ("x", "y"))
    gram = jnp.zeros((16, cells), jnp.float32)
    q, sent, gram = combine(0, met, gram, [])
    pieces, fields = [q], []
    for j in range(1, KRYLOV + 1):
        fields.append(spread(sent))
        if j == KRYLOV:
            outer = lax.ppermute(jnp.stack(pieces), ALL, TO_OUTER)
        met = exchange(
            apply_rates(core_id, rates, got_rates, weights, fields, False), ("x", "y")
        )
        if j < KRYLOV:
            q, sent, gram = combine(j, met, gram, pieces)
            pieces.append(q)
        else:
            dots, gram = combine(j, met, gram, pieces)
    dots = dots + lax.ppermute(dots, "k", SWAP)
    dots = exchange(jnp.broadcast_to(dots[None], (NZ * NX * NY, *dots.shape)), ("z", "x", "y"))
    return pl.pallas_call(
        finish_kernel,
        out_shape=jax.ShapeDtypeStruct(populations.shape, jnp.float32),
        name="finish",
    )(populations, outer, gram, dots)


def solution(mesh):
    named = Mesh(mesh.devices.reshape(NZ, NK, NX, NY), ALL)
    placed = (P(None, ("z", "k"), ("x", "y")), P(ALL, None), P(), P())
    return jax.shard_map(
        body, mesh=named, in_specs=placed, out_specs=P(ALL, None), check_vma=False
    )
```

```python
import math

import jax
import jax.numpy as jnp
from jax import lax
from jax.experimental import pallas as pl
from jax.experimental.pallas import tpu as pltpu
from jax.sharding import Mesh, PartitionSpec as P

KRYLOV = 4
TAYLOR = 8
TERMS = 6

epsilon = 1e-06
step_size = 1.0

NZ, NK, NX, NY = 4, 2, 4, 4
ALL = ("z", "k", "x", "y")
SUB = 64
HALF = NX * SUB
COLS = NK * HALF
EXTRA = 16
WIRE = jnp.float16


def device(z, k, x, y):
    return ((z * NK + k) * NX + x) * NY + y


TO_INNER = [
    (device(z, k, x, y), device(z, (k + x) % 2, y, 2 * k + x // 2))
    for z in range(NZ)
    for k in range(NK)
    for x in range(NX)
    for y in range(NY)
]
TO_OUTER = [(b, a) for a, b in TO_INNER]
SWAP = [(0, 1), (1, 0)]
SPREAD = [
    [
        ((z * NK + k) * NX + x, (((x + 2 * k + t) % NZ) * NK + k) * NX + z)
        for z in range(NZ)
        for k in range(NK)
        for x in range(NX)
    ]
    for t in range(2)
]


def exponent(value):
    return jnp.floor(jnp.log2(jnp.maximum(jnp.abs(value), 1e-30)))


def solve(gram, count):
    g = lambda m, n: gram[(min(m, n), max(m, n))]
    scale = jnp.sqrt(g(1, 1) + epsilon)
    combos = {1: {1: 1.0 / scale}}
    hess = {(1, 0): scale}
    for j in range(1, count):
        d = {j + 1: None}
        for m in range(1, j + 1):
            d[m] = 0.0
        for i in range(1, j + 1):
            h = 0.0
            for m, c in combos[i].items():
                h = h + c * g(m, j + 1)
            hess[(i, j)] = h
            for m, c in combos[i].items():
                d[m] = d[m] - h * c
        square = g(j + 1, j + 1)
        for m in range(1, j + 1):
            inner = 2.0 * g(m, j + 1)
            for n in range(1, j + 1):
                inner = inner + d[n] * g(m, n)
            square = square + d[m] * inner
        length = jnp.sqrt(jnp.maximum(square, 0.0) + epsilon)
        hess[(j + 1, j)] = length
        inv = 1.0 / length
        combos[j + 1] = {m: (inv if m == j + 1 else d[m] * inv) for m in d}
    return combos, hess


def matmul_kernel(n_fields, exact, at_ref, kept_ref, got_ref, w_ref, *refs):
    own_refs, other_refs = refs[:n_fields], refs[n_fields : 2 * n_fields]
    out_ref, x_ref, extra_ref = refs[2 * n_fields :]
    step = pl.program_id(0)
    core, place, side = at_ref[0], at_ref[1], at_ref[2]
    cells = w_ref.shape[1]

    @pl.when(step == 0)
    def _():
        for ref, k in ((own_refs[-1], core), (other_refs[-1], 1 - core)):
            for t in range(2):
                x = (place + 2 * NZ - 2 * k - t) % NX
                for o in range(2):
                    half = (k + o + side) % 2
                    rows = pl.ds(pl.multiple_of(half * HALF + x * SUB, SUB), SUB)
                    value = ref[t, o]
                    high = value.astype(jnp.bfloat16)
                    x_ref[rows, pl.ds(0, cells)] = high
                    if not exact:
                        low = (value - high.astype(jnp.float32)).astype(jnp.bfloat16)
                        x_ref[rows, pl.ds(cells, cells)] = low
        extra_ref[...] = jnp.zeros_like(extra_ref)
        if not exact:
            for m in range(n_fields):
                total = jnp.zeros((8, cells), jnp.float32)
                for a_ref, b_ref in ((own_refs[m], own_refs[-1]), (other_refs[m], other_refs[-1])):
                    product = a_ref[...] * b_ref[...]
                    total = total + jnp.sum(product.reshape(HALF // 8, 8, cells), axis=0)
                total = jnp.sum(total, axis=0, keepdims=True)
                power = exponent(total)
                total = total * jnp.exp2(-power)
                high = total.astype(jnp.bfloat16).astype(jnp.float32)
                extra_ref[pl.ds(3 * m + 1, 1), :] = power
                extra_ref[pl.ds(3 * m + 2, 1), :] = high
                extra_ref[pl.ds(3 * m + 3, 1), :] = (total - high) * 256.0

    def part(rates):
        total = None
        for j in range(TERMS):
            product = jnp.dot(rates[j, 0], x_ref[...], preferred_element_type=jnp.float32)
            if not exact:
                product = product[:, :cells] + product[:, cells:]
            product = w_ref[pl.ds(j, 1), :] * product
            total = product if total is None else total + product
        for x in range(NX):
            block = total[x * SUB : (x + 1) * SUB, :]
            power = exponent(jnp.max(jnp.abs(block), axis=0, keepdims=True))
            out_ref[x, 0, pl.ds(0, SUB), :] = block * jnp.exp2(-power)
            out_ref[x, 0, pl.ds(SUB, EXTRA), :] = extra_ref[...]
            out_ref[x, 0, pl.ds(SUB, 1), :] = power

    @pl.when(step < 2)
    def _():
        part(kept_ref)

    @pl.when(step >= 2)
    def _():
        part(got_ref)


def apply_rates(at, kept, got, weights, fields, exact):
    cells = weights.shape[1]
    rows = SUB + EXTRA
    whole = lambda a: pl.BlockSpec(a.shape, lambda g, at: (0,) * a.ndim)
    own, other = [f[0] for f in fields], [f[1] for f in fields]
    block = (TERMS, 1, HALF, COLS)

    def kernel(*refs):
        matmul_kernel(len(fields), exact, *refs)

    out = pl.pallas_call(
        kernel,
        out_shape=jax.ShapeDtypeStruct((NX, NY, rows, cells), jnp.float32),
        grid_spec=pltpu.PrefetchScalarGridSpec(
            num_scalar_prefetch=1,
            grid=(NY,),
            in_specs=[
                pl.BlockSpec(block, lambda g, at: (0, 2 * jnp.minimum(g, 1), 0, 0)),
                pl.BlockSpec(block, lambda g, at: (0, jnp.maximum(g - 2, 0), 0, 0)),
                whole(weights),
                *[whole(a) for a in own],
                *[whole(a) for a in other],
            ],
            out_specs=pl.BlockSpec(
                (NX, 1, rows, cells), lambda g, at: (0, (g + 2 * at[0]) % NY, 0, 0)
            ),
            scratch_shapes=[
                pltpu.VMEM((COLS, cells if exact else 2 * cells), jnp.bfloat16),
                pltpu.VMEM((EXTRA, cells), jnp.float32),
            ],
        ),
        name="rates",
    )(at, kept, got, weights, *own, *other)
    return out.reshape(NX * NY, rows, cells)


def combine_kernel(j, got_ref, gram_ref, *refs):
    q_refs, outs = refs[:j], refs[j:]
    cells = got_ref.shape[2]
    fresh, inner = None, [None] * j
    for b in range(NX * NY):
        extra = got_ref[b, pl.ds(SUB, EXTRA), :]
        value = got_ref[b, pl.ds(0, SUB), :] * jnp.exp2(extra[:1])
        fresh = value if fresh is None else fresh + value
        for m in range(j):
            value = extra[3 * m + 2 : 3 * m + 3] + extra[3 * m + 3 : 3 * m + 4] * (1.0 / 256.0)
            value = value * jnp.exp2(extra[3 * m + 1 : 3 * m + 2])
            inner[m] = value if inner[m] is None else inner[m] + value
    gram_out = outs[-1]
    gram = {}
    if j > 0:
        gram_out[...] = gram_ref[...]
        for m in range(1, j + 1):
            for n in range(m, j):
                gram[(m, n)] = gram_ref[pl.ds(4 * (m - 1) + n - 1, 1), :]
            row = inner[m - 1]
            gram[(m, j)] = row
            gram_out[pl.ds(4 * (m - 1) + j - 1, 1), :] = row
        _, hess = solve(gram, j)
        for i in range(1, j):
            fresh = fresh - hess[(i, j - 1)] * q_refs[i][...]
        fresh = fresh * (1.0 / hess[(j, j - 1)])
    else:
        gram_out[...] = jnp.zeros_like(gram_out)
    if j < KRYLOV:
        outs[0][...] = fresh
    else:
        dots = outs[0]
        lanes = dots.shape[1]
        for m in range(1, KRYLOV + 1):
            row = jnp.sum(q_refs[m - 1][...] * fresh, axis=0, keepdims=True)
            dots[pl.ds(m - 1, 1), :] = row[:, :lanes]
            dots[pl.ds(KRYLOV + m - 1, 1), :] = row[:, lanes:]


def combine(j, got, gram, fields):
    cells = got.shape[2]

    def kernel(*refs):
        combine_kernel(j, *refs)

    if j < KRYLOV:
        outs = (jax.ShapeDtypeStruct((SUB, cells), jnp.float32),)
    else:
        outs = (jax.ShapeDtypeStruct((2 * KRYLOV, cells // 2), jnp.float32),)
    return pl.pallas_call(
        kernel,
        out_shape=(*outs, jax.ShapeDtypeStruct(gram.shape, jnp.float32)),
        name=f"combine{j}",
    )(got, gram, *fields)


def finish_kernel(p_ref, q_ref, gram_ref, dots_ref, out_ref):
    gram = {}
    for m in range(1, KRYLOV + 1):
        for n in range(m, KRYLOV + 1):
            gram[(m, n)] = gram_ref[pl.ds(4 * (m - 1) + n - 1, 1), :]
    dots = jnp.sum(dots_ref[...], axis=0)
    last = {
        m: jnp.concatenate([dots[m - 1 : m], dots[KRYLOV + m - 1 : KRYLOV + m]], axis=1)
        for m in range(1, KRYLOV + 1)
    }
    combos, hess = solve(gram, KRYLOV)
    for i in range(1, KRYLOV + 1):
        h = 0.0
        for m, c in combos[i].items():
            h = h + c * last[m]
        hess[(i, KRYLOV)] = h
    zero = jnp.zeros_like(gram[(1, 1)])
    unit = [zero + 1.0] + [zero] * (KRYLOV - 1)
    coeffs = [u / float(math.factorial(TAYLOR + 1)) for u in unit]
    for k in range(TAYLOR - 1, -1, -1):
        fresh = []
        for i in range(1, KRYLOV + 1):
            value = unit[i - 1] / float(math.factorial(k + 1))
            for j in range(max(i - 1, 1), KRYLOV + 1):
                value = value + step_size * hess[(i, j)] * coeffs[j - 1]
            fresh.append(value)
        coeffs = fresh
    out = p_ref[...]
    for m in range(1, KRYLOV + 1):
        factor = 0.0
        for i in range(m, KRYLOV + 1):
            factor = factor + coeffs[i - 1] * combos[i][m]
        out = out + step_size * hess[(1, 0)] * factor * q_ref[m - 1]
    out_ref[...] = out


def body(rate_terms, populations, temp_bins, bin_coeffs):
    core = lax.axis_index("k")
    n_bins = bin_coeffs.shape[0]
    cells = populations.shape[1]
    exchange = lambda v, axes: lax.all_to_all(v, axes, 0, 0, tiled=True)

    rates = rate_terms.reshape(TERMS, 2 * NK, HALF, COLS)
    away = rate_terms.reshape(TERMS, 2, NK, HALF, COLS)[:, :, 1]
    got_rates = lax.ppermute(away, "k", SWAP)

    onehot = (temp_bins[:, None] == jnp.arange(n_bins, dtype=jnp.int32)[None, :]).astype(
        jnp.float32
    )
    weights = jnp.dot(onehot, bin_coeffs, precision=lax.Precision.HIGHEST)
    weights = jnp.pad(weights.T, ((0, 2), (0, 0)))
    at = jnp.stack([core, lax.axis_index("z"), lax.axis_index("y") // 2]).astype(jnp.int32)

    def spread(piece):
        both = jnp.stack([piece, lax.ppermute(piece, "k", SWAP)])
        own = jnp.stack([lax.ppermute(both, ("z", "k", "x"), pairs) for pairs in SPREAD])
        other = lax.ppermute(own, "k", SWAP)
        return own.astype(jnp.float32), other.astype(jnp.float32)

    def reduce(partial):
        return exchange(partial.astype(WIRE), ("x", "y")).astype(jnp.float32)

    piece = lax.ppermute(populations.astype(jnp.bfloat16), ALL, TO_INNER)
    met = reduce(apply_rates(at, rates, got_rates, weights, [spread(piece)], True))
    gram = jnp.zeros((16, cells), jnp.float32)
    q, gram = combine(0, met, gram, [])
    pieces, fields = [q], []
    for j in range(1, KRYLOV + 1):
        fields.append(spread(q.astype(WIRE)))
        if j == KRYLOV:
            outer = lax.ppermute(jnp.stack(pieces), ALL, TO_OUTER)
        met = reduce(apply_rates(at, rates, got_rates, weights, fields, False))
        if j < KRYLOV:
            q, gram = combine(j, met, gram, pieces)
            pieces.append(q)
        else:
            dots, gram = combine(j, met, gram, pieces)
    dots = dots + lax.ppermute(dots, "k", SWAP)
    dots = exchange(jnp.broadcast_to(dots[None], (NZ * NX * NY, *dots.shape)), ("z", "x", "y"))
    return pl.pallas_call(
        finish_kernel,
        out_shape=jax.ShapeDtypeStruct(populations.shape, jnp.float32),
        name="finish",
    )(populations, outer, gram, dots)


def solution(mesh):
    named = Mesh(mesh.devices.reshape(NZ, NK, NX, NY), ALL)
    placed = (P(None, ("z", "k"), ("x", "y")), P(ALL, None), P(), P())
    return jax.shard_map(
        body, mesh=named, in_specs=placed, out_specs=P(ALL, None), check_vma=False
    )
```

```python
import math

import jax
import jax.numpy as jnp
from jax import lax
from jax.experimental import pallas as pl
from jax.experimental.pallas import tpu as pltpu
from jax.sharding import Mesh, PartitionSpec as P

KRYLOV = 4
TAYLOR = 8
TERMS = 6

epsilon = 1e-06
step_size = 1.0

NZ, NK, NX, NY = 4, 2, 4, 4
ALL = ("z", "k", "x", "y")
SUB = 64
HALF = NX * SUB
COLS = NK * HALF
EXTRA = 16
WIRE = jnp.float16


def device(z, k, x, y):
    return ((z * NK + k) * NX + x) * NY + y


TO_INNER = [
    (device(z, k, x, y), device(z, (k + x) % 2, y, 2 * k + x // 2))
    for z in range(NZ)
    for k in range(NK)
    for x in range(NX)
    for y in range(NY)
]
TO_OUTER = [(b, a) for a, b in TO_INNER]
SWAP = [(0, 1), (1, 0)]
SPREAD = [
    [
        ((z * NK + k) * NX + x, (((x + 2 * k + t) % NZ) * NK + k) * NX + z)
        for z in range(NZ)
        for k in range(NK)
        for x in range(NX)
    ]
    for t in range(2)
]


def exponent(value):
    return jnp.floor(jnp.log2(jnp.maximum(jnp.abs(value), 1e-30)))


def solve(gram, count):
    g = lambda m, n: gram[(min(m, n), max(m, n))]
    scale = jnp.sqrt(g(1, 1) + epsilon)
    combos = {1: {1: 1.0 / scale}}
    hess = {(1, 0): scale}
    for j in range(1, count):
        d = {j + 1: None}
        for m in range(1, j + 1):
            d[m] = 0.0
        for i in range(1, j + 1):
            h = 0.0
            for m, c in combos[i].items():
                h = h + c * g(m, j + 1)
            hess[(i, j)] = h
            for m, c in combos[i].items():
                d[m] = d[m] - h * c
        square = g(j + 1, j + 1)
        for m in range(1, j + 1):
            inner = 2.0 * g(m, j + 1)
            for n in range(1, j + 1):
                inner = inner + d[n] * g(m, n)
            square = square + d[m] * inner
        length = jnp.sqrt(jnp.maximum(square, 0.0) + epsilon)
        hess[(j + 1, j)] = length
        inv = 1.0 / length
        combos[j + 1] = {m: (inv if m == j + 1 else d[m] * inv) for m in d}
    return combos, hess


def call(kernel, name, outs, *operands, scratch=()):
    vmem = pl.BlockSpec(memory_space=pltpu.VMEM)
    return pl.pallas_call(
        kernel,
        out_shape=outs,
        in_specs=[
            pl.BlockSpec(memory_space=pltpu.SMEM) if a.dtype == jnp.int32 else vmem for a in operands
        ],
        out_specs=jax.tree.map(lambda _: vmem, outs),
        scratch_shapes=scratch,
        compiler_params=pltpu.CompilerParams(vmem_limit_bytes=16 << 20),
        name=name,
    )(*operands)


def matmul_kernel(n_fields, exact, at_ref, kept_ref, got_ref, w_ref, *refs):
    own_refs, other_refs = refs[:n_fields], refs[n_fields : 2 * n_fields]
    out_ref, x_ref, extra_ref = refs[2 * n_fields :]
    core, place, side = at_ref[0], at_ref[1], at_ref[2]
    cells = w_ref.shape[1]

    for ref, k in ((own_refs[-1], core), (other_refs[-1], 1 - core)):
        for t in range(2):
            x = (place + 2 * NZ - 2 * k - t) % NX
            for o in range(2):
                half = (k + o + side) % 2
                rows = pl.ds(pl.multiple_of(half * HALF + x * SUB, SUB), SUB)
                value = ref[t, o].astype(jnp.float32)
                high = value.astype(jnp.bfloat16)
                x_ref[rows, pl.ds(0, cells)] = high
                if not exact:
                    low = (value - high.astype(jnp.float32)).astype(jnp.bfloat16)
                    x_ref[rows, pl.ds(cells, cells)] = low
    extra_ref[...] = jnp.zeros_like(extra_ref)
    if not exact:
        for m in range(n_fields):
            total = jnp.zeros((8, cells), jnp.float32)
            for a_ref, b_ref in ((own_refs[m], own_refs[-1]), (other_refs[m], other_refs[-1])):
                product = a_ref[...] * b_ref[...]
                total = total + jnp.sum(product.reshape(HALF // 8, 8, cells), axis=0)
            total = jnp.sum(total, axis=0, keepdims=True)
            power = exponent(total)
            total = total * jnp.exp2(-power)
            high = total.astype(jnp.bfloat16).astype(jnp.float32)
            extra_ref[pl.ds(3 * m + 1, 1), :] = power
            extra_ref[pl.ds(3 * m + 2, 1), :] = high
            extra_ref[pl.ds(3 * m + 3, 1), :] = (total - high) * 256.0

    for g in range(NY):
        y = (g + 2 * core) % NY
        total = None
        for j in range(TERMS):
            rates = kept_ref[j, 2 * g] if g < 2 else got_ref[j, g - 2]
            product = jnp.dot(rates, x_ref[...], preferred_element_type=jnp.float32)
            if not exact:
                product = product[:, :cells] + product[:, cells:]
            product = w_ref[pl.ds(j, 1), :] * product
            total = product if total is None else total + product
        for x in range(NX):
            block = total[x * SUB : (x + 1) * SUB, :]
            power = exponent(jnp.max(jnp.abs(block), axis=0, keepdims=True))
            out_ref[x, y, pl.ds(0, SUB), :] = block * jnp.exp2(-power)
            out_ref[x, y, pl.ds(SUB, EXTRA), :] = extra_ref[...]
            out_ref[x, y, pl.ds(SUB, 1), :] = power


def apply_rates(at, kept, got, weights, fields, exact):
    cells = weights.shape[1]
    rows = SUB + EXTRA
    own, other = [f[0] for f in fields], [f[1] for f in fields]

    def kernel(*refs):
        matmul_kernel(len(fields), exact, *refs)

    out = call(
        kernel,
        "rates",
        jax.ShapeDtypeStruct((NX, NY, rows, cells), jnp.float32),
        at,
        kept,
        got,
        weights,
        *own,
        *other,
        scratch=[
            pltpu.VMEM((COLS, cells if exact else 2 * cells), jnp.bfloat16),
            pltpu.VMEM((EXTRA, cells), jnp.float32),
        ],
    )
    return out.reshape(NX * NY, rows, cells)


def combine_kernel(j, got_ref, gram_ref, *refs):
    q_refs, outs = refs[:j], refs[j:]
    cells = got_ref.shape[2]
    fresh, inner = None, [None] * j
    for b in range(NX * NY):
        extra = got_ref[b, pl.ds(SUB, EXTRA), :]
        value = got_ref[b, pl.ds(0, SUB), :] * jnp.exp2(extra[:1])
        fresh = value if fresh is None else fresh + value
        for m in range(j):
            value = extra[3 * m + 2 : 3 * m + 3] + extra[3 * m + 3 : 3 * m + 4] * (1.0 / 256.0)
            value = value * jnp.exp2(extra[3 * m + 1 : 3 * m + 2])
            inner[m] = value if inner[m] is None else inner[m] + value
    gram_out = outs[-1]
    gram = {}
    if j > 0:
        gram_out[...] = gram_ref[...]
        for m in range(1, j + 1):
            for n in range(m, j):
                gram[(m, n)] = gram_ref[pl.ds(4 * (m - 1) + n - 1, 1), :]
            row = inner[m - 1]
            gram[(m, j)] = row
            gram_out[pl.ds(4 * (m - 1) + j - 1, 1), :] = row
        _, hess = solve(gram, j)
        for i in range(1, j):
            fresh = fresh - hess[(i, j - 1)] * q_refs[i][...]
        fresh = fresh * (1.0 / hess[(j, j - 1)])
    else:
        gram_out[...] = jnp.zeros_like(gram_out)
    if j < KRYLOV:
        outs[0][...] = fresh
    else:
        dots = outs[0]
        lanes = dots.shape[1]
        for m in range(1, KRYLOV + 1):
            row = jnp.sum(q_refs[m - 1][...] * fresh, axis=0, keepdims=True)
            dots[pl.ds(m - 1, 1), :] = row[:, :lanes]
            dots[pl.ds(KRYLOV + m - 1, 1), :] = row[:, lanes:]


def combine(j, got, gram, fields):
    cells = got.shape[2]

    def kernel(*refs):
        combine_kernel(j, *refs)

    if j < KRYLOV:
        outs = (jax.ShapeDtypeStruct((SUB, cells), jnp.float32),)
    else:
        outs = (jax.ShapeDtypeStruct((2 * KRYLOV, cells // 2), jnp.float32),)
    outs = (*outs, jax.ShapeDtypeStruct(gram.shape, jnp.float32))
    return call(kernel, f"combine{j}", outs, got, gram, *fields)


def finish_kernel(p_ref, q_ref, gram_ref, dots_ref, out_ref):
    gram = {}
    for m in range(1, KRYLOV + 1):
        for n in range(m, KRYLOV + 1):
            gram[(m, n)] = gram_ref[pl.ds(4 * (m - 1) + n - 1, 1), :]
    dots = jnp.sum(dots_ref[...], axis=0)
    last = {
        m: jnp.concatenate([dots[m - 1 : m], dots[KRYLOV + m - 1 : KRYLOV + m]], axis=1)
        for m in range(1, KRYLOV + 1)
    }
    combos, hess = solve(gram, KRYLOV)
    for i in range(1, KRYLOV + 1):
        h = 0.0
        for m, c in combos[i].items():
            h = h + c * last[m]
        hess[(i, KRYLOV)] = h
    zero = jnp.zeros_like(gram[(1, 1)])
    unit = [zero + 1.0] + [zero] * (KRYLOV - 1)
    coeffs = [u / float(math.factorial(TAYLOR + 1)) for u in unit]
    for k in range(TAYLOR - 1, -1, -1):
        fresh = []
        for i in range(1, KRYLOV + 1):
            value = unit[i - 1] / float(math.factorial(k + 1))
            for j in range(max(i - 1, 1), KRYLOV + 1):
                value = value + step_size * hess[(i, j)] * coeffs[j - 1]
            fresh.append(value)
        coeffs = fresh
    out = p_ref[...]
    for m in range(1, KRYLOV + 1):
        factor = 0.0
        for i in range(m, KRYLOV + 1):
            factor = factor + coeffs[i - 1] * combos[i][m]
        out = out + step_size * hess[(1, 0)] * factor * q_ref[m - 1]
    out_ref[...] = out


def body(rate_terms, populations, temp_bins, bin_coeffs):
    core = lax.axis_index("k")
    n_bins = bin_coeffs.shape[0]
    cells = populations.shape[1]
    exchange = lambda v, axes: lax.all_to_all(v, axes, 0, 0, tiled=True)

    rates = rate_terms.reshape(TERMS, 2 * NK, HALF, COLS)
    rates = pltpu.with_memory_space_constraint(rates, pltpu.VMEM)
    away = rate_terms.reshape(TERMS, 2, NK, HALF, COLS)[:, :, 1]
    got_rates = lax.ppermute(away, "k", SWAP)
    got_rates = pltpu.with_memory_space_constraint(got_rates, pltpu.VMEM)

    onehot = (temp_bins[:, None] == jnp.arange(n_bins, dtype=jnp.int32)[None, :]).astype(
        jnp.float32
    )
    weights = jnp.dot(onehot, bin_coeffs, precision=lax.Precision.HIGHEST)
    weights = jnp.pad(weights.T, ((0, 2), (0, 0)))
    at = jnp.stack([core, lax.axis_index("z"), lax.axis_index("y") // 2]).astype(jnp.int32)

    def spread(piece):
        both = jnp.stack([piece, lax.ppermute(piece, "k", SWAP)])
        own = jnp.stack([lax.ppermute(both, ("z", "k", "x"), pairs) for pairs in SPREAD])
        other = lax.ppermute(own, "k", SWAP)
        return own.astype(jnp.float32), other.astype(jnp.float32)

    def reduce(partial):
        return exchange(partial.astype(WIRE), ("x", "y")).astype(jnp.float32)

    piece = lax.ppermute(populations.astype(jnp.bfloat16), ALL, TO_INNER)
    met = reduce(apply_rates(at, rates, got_rates, weights, [spread(piece)], True))
    gram = jnp.zeros((16, cells), jnp.float32)
    q, gram = combine(0, met, gram, [])
    pieces, fields = [q], []
    for j in range(1, KRYLOV + 1):
        fields.append(spread(q.astype(WIRE)))
        if j == KRYLOV:
            outer = lax.ppermute(jnp.stack(pieces), ALL, TO_OUTER)
        met = reduce(apply_rates(at, rates, got_rates, weights, fields, False))
        if j < KRYLOV:
            q, gram = combine(j, met, gram, pieces)
            pieces.append(q)
        else:
            dots, gram = combine(j, met, gram, pieces)
    dots = dots + lax.ppermute(dots, "k", SWAP)
    dots = exchange(jnp.broadcast_to(dots[None], (NZ * NX * NY, *dots.shape)), ("z", "x", "y"))
    out = jax.ShapeDtypeStruct(populations.shape, jnp.float32)
    return call(finish_kernel, "finish", out, populations, outer, gram, dots)


def solution(mesh):
    named = Mesh(mesh.devices.reshape(NZ, NK, NX, NY), ALL)
    placed = (P(None, ("z", "k"), ("x", "y")), P(ALL, None), P(), P())
    return jax.shard_map(
        body, mesh=named, in_specs=placed, out_specs=P(ALL, None), check_vma=False
    )
```

```python
import math

import jax
import jax.numpy as jnp
from jax import lax
from jax.experimental import pallas as pl
from jax.experimental.pallas import tpu as pltpu
from jax.sharding import Mesh, PartitionSpec as P

KRYLOV = 4
TAYLOR = 8
TERMS = 6

epsilon = 1e-06
step_size = 1.0

NZ, NK, NX, NY = 4, 2, 4, 4
ALL = ("z", "k", "x", "y")
SUB = 64
HALF = NX * SUB
COLS = NK * HALF
WIRE = jnp.float16


def device(z, k, x, y):
    return ((z * NK + k) * NX + x) * NY + y


TO_OUTER = [
    (device(z, (k + x) % 2, y, 2 * k + x // 2), device(z, k, x, y))
    for z in range(NZ)
    for k in range(NK)
    for x in range(NX)
    for y in range(NY)
]
FIRST = [
    [
        (device(z, k, x, y), device((y + s) % NZ, x % 2, z, 2 * k + x // 2))
        for z in range(NZ)
        for k in range(NK)
        for x in range(NX)
        for y in range(NY)
    ]
    for s in range(NZ)
]
SWAP = [(0, 1), (1, 0)]
SPREAD = [
    [
        ((z * NK + k) * NX + x, (((x + 2 * k + t) % NZ) * NK + k) * NX + z)
        for z in range(NZ)
        for k in range(NK)
        for x in range(NX)
    ]
    for t in range(2)
]


def exponent(value):
    return jnp.floor(jnp.log2(jnp.maximum(jnp.abs(value), 1e-30)))


def solve(gram, count):
    g = lambda m, n: gram[(min(m, n), max(m, n))]
    scale = jnp.sqrt(g(1, 1) + epsilon)
    combos = {1: {1: 1.0 / scale}}
    hess = {(1, 0): scale}
    for j in range(1, count):
        d = {j + 1: None}
        for m in range(1, j + 1):
            d[m] = 0.0
        for i in range(1, j + 1):
            h = 0.0
            for m, c in combos[i].items():
                h = h + c * g(m, j + 1)
            hess[(i, j)] = h
            for m, c in combos[i].items():
                d[m] = d[m] - h * c
        square = g(j + 1, j + 1)
        for m in range(1, j + 1):
            inner = 2.0 * g(m, j + 1)
            for n in range(1, j + 1):
                inner = inner + d[n] * g(m, n)
            square = square + d[m] * inner
        length = jnp.sqrt(jnp.maximum(square, 0.0) + epsilon)
        hess[(j + 1, j)] = length
        inv = 1.0 / length
        combos[j + 1] = {m: (inv if m == j + 1 else d[m] * inv) for m in d}
    return combos, hess


def call(kernel, name, outs, *operands, scratch=()):
    vmem = pl.BlockSpec(memory_space=pltpu.VMEM)
    return pl.pallas_call(
        kernel,
        out_shape=outs,
        in_specs=[
            pl.BlockSpec(memory_space=pltpu.SMEM) if a.dtype == jnp.int32 else vmem for a in operands
        ],
        out_specs=jax.tree.map(lambda _: vmem, outs),
        scratch_shapes=scratch,
        compiler_params=pltpu.CompilerParams(vmem_limit_bytes=16 << 20),
        name=name,
    )(*operands)


def away_kernel(rates_ref, out_ref, sems):
    copies = [
        pltpu.make_async_copy(rates_ref.at[:, h, 1], out_ref.at[:, h], sems.at[h]) for h in range(2)
    ]
    for copy in copies:
        copy.start()
    for copy in copies:
        copy.wait()


def give_away(halves):
    return pl.pallas_call(
        away_kernel,
        out_shape=jax.ShapeDtypeStruct((TERMS, 2, HALF, COLS), halves.dtype),
        in_specs=[pl.BlockSpec(memory_space=pl.ANY)],
        out_specs=pl.BlockSpec(memory_space=pl.ANY),
        scratch_shapes=[pltpu.SemaphoreType.DMA((2,))],
        compiler_params=pltpu.CompilerParams(vmem_limit_bytes=56 << 20),
        name="away",
    )(halves)


def extras(n_fields):
    return (1 + 3 * n_fields + 7) // 8 * 8


def matmul_kernel(n_fields, exact, at_ref, kept_ref, got_ref, w_ref, *refs):
    own_refs, other_refs = refs[:n_fields], refs[n_fields : 2 * n_fields]
    out_ref, x_ref = refs[2 * n_fields :][:2]
    core, place, side = at_ref[0], at_ref[1], at_ref[2]
    cells = w_ref.shape[1]

    for ref, k in ((own_refs[-1], core), (other_refs[-1], 1 - core)):
        for i in range(NX):
            if exact:
                x, half, value = (place + NZ - i) % NX, k, ref[i]
            else:
                t, o = divmod(i, 2)
                x, half = (place + 2 * NZ - 2 * k - t) % NX, (k + o + side) % 2
                value = ref[t, o]
            rows = pl.ds(pl.multiple_of(half * HALF + x * SUB, SUB), SUB)
            high = value.astype(jnp.bfloat16)
            x_ref[rows, pl.ds(0, cells)] = high
            if not exact:
                low = (value - high.astype(jnp.float32)).astype(jnp.bfloat16)
                x_ref[rows, pl.ds(cells, cells)] = low
    if not exact:
        extra_ref = refs[-1]
        extra_ref[...] = jnp.zeros_like(extra_ref)
        for m in range(n_fields):
            total = jnp.zeros((8, cells), jnp.float32)
            for a_ref, b_ref in ((own_refs[m], own_refs[-1]), (other_refs[m], other_refs[-1])):
                product = a_ref[...] * b_ref[...]
                total = total + jnp.sum(product.reshape(HALF // 8, 8, cells), axis=0)
            total = jnp.sum(total, axis=0, keepdims=True)
            power = exponent(total)
            total = total * jnp.exp2(-power)
            high = total.astype(jnp.bfloat16).astype(jnp.float32)
            extra_ref[pl.ds(3 * m + 1, 1), :] = power
            extra_ref[pl.ds(3 * m + 2, 1), :] = high
            extra_ref[pl.ds(3 * m + 3, 1), :] = (total - high) * 256.0

    for g in range(NY):
        y = (g + 2 * core) % NY
        total = None
        for j in range(TERMS):
            rates = kept_ref[j, g, 0] if g < 2 else got_ref[j, g - 2]
            product = jnp.dot(rates, x_ref[...], preferred_element_type=jnp.float32)
            if not exact:
                product = product[:, :cells] + product[:, cells:]
            product = w_ref[pl.ds(j, 1), :] * product
            total = product if total is None else total + product
        for x in range(NX):
            block = total[x * SUB : (x + 1) * SUB, :]
            if exact:
                out_ref[x, y] = block
                continue
            power = exponent(jnp.max(jnp.abs(block), axis=0, keepdims=True))
            out_ref[x, y, pl.ds(0, SUB), :] = block * jnp.exp2(-power)
            out_ref[x, y, pl.ds(SUB, extra_ref.shape[0]), :] = extra_ref[...]
            out_ref[x, y, pl.ds(SUB, 1), :] = power


def apply_rates(at, kept, got, weights, fields, exact):
    cells = weights.shape[1]
    more = 0 if exact else extras(len(fields))
    rows = SUB + more
    own, other = [f[0] for f in fields], [f[1] for f in fields]

    def kernel(*refs):
        matmul_kernel(len(fields), exact, *refs)

    out = call(
        kernel,
        "rates",
        jax.ShapeDtypeStruct((NX, NY, rows, cells), jnp.float32),
        at,
        kept,
        got,
        weights,
        *own,
        *other,
        scratch=[pltpu.VMEM((COLS, cells if exact else 2 * cells), jnp.bfloat16)]
        + ([] if exact else [pltpu.VMEM((more, cells), jnp.float32)]),
    )
    return out.reshape(NX * NY, rows, cells)


def combine_kernel(j, got_ref, gram_ref, *refs):
    q_refs, outs = refs[:j], refs[j:]
    cells = got_ref.shape[2]
    fresh, inner = None, [None] * j
    for b in range(NX * NY):
        value = got_ref[b, pl.ds(0, SUB), :]
        if j > 0:
            extra = got_ref[b, pl.ds(SUB, extras(j)), :]
            value = value * jnp.exp2(extra[:1])
        fresh = value if fresh is None else fresh + value
        for m in range(j):
            value = extra[3 * m + 2 : 3 * m + 3] + extra[3 * m + 3 : 3 * m + 4] * (1.0 / 256.0)
            value = value * jnp.exp2(extra[3 * m + 1 : 3 * m + 2])
            inner[m] = value if inner[m] is None else inner[m] + value
    gram_out = outs[-1]
    gram = {}
    if j > 0:
        gram_out[...] = gram_ref[...]
        for m in range(1, j + 1):
            for n in range(m, j):
                gram[(m, n)] = gram_ref[pl.ds(4 * (m - 1) + n - 1, 1), :]
            row = inner[m - 1]
            gram[(m, j)] = row
            gram_out[pl.ds(4 * (m - 1) + j - 1, 1), :] = row
        _, hess = solve(gram, j)
        for i in range(1, j):
            fresh = fresh - hess[(i, j - 1)] * q_refs[i][...]
        fresh = fresh * (1.0 / hess[(j, j - 1)])
    else:
        gram_out[...] = jnp.zeros_like(gram_out)
    if j < KRYLOV:
        outs[0][...] = fresh
    else:
        dots = outs[0]
        lanes = dots.shape[1]
        for m in range(1, KRYLOV + 1):
            row = jnp.sum(q_refs[m - 1][...] * fresh, axis=0, keepdims=True)
            dots[pl.ds(m - 1, 1), :] = row[:, :lanes]
            dots[pl.ds(KRYLOV + m - 1, 1), :] = row[:, lanes:]


def combine(j, got, gram, fields):
    cells = got.shape[2]

    def kernel(*refs):
        combine_kernel(j, *refs)

    if j < KRYLOV:
        outs = (jax.ShapeDtypeStruct((SUB, cells), jnp.float32),)
    else:
        outs = (jax.ShapeDtypeStruct((2 * KRYLOV, cells // 2), jnp.float32),)
    outs = (*outs, jax.ShapeDtypeStruct(gram.shape, jnp.float32))
    return call(kernel, f"combine{j}", outs, got, gram, *fields)


def finish_kernel(p_ref, q_ref, gram_ref, dots_ref, out_ref):
    gram = {}
    for m in range(1, KRYLOV + 1):
        for n in range(m, KRYLOV + 1):
            gram[(m, n)] = gram_ref[pl.ds(4 * (m - 1) + n - 1, 1), :]
    dots = jnp.sum(dots_ref[...], axis=0)
    last = {
        m: jnp.concatenate([dots[m - 1 : m], dots[KRYLOV + m - 1 : KRYLOV + m]], axis=1)
        for m in range(1, KRYLOV + 1)
    }
    combos, hess = solve(gram, KRYLOV)
    for i in range(1, KRYLOV + 1):
        h = 0.0
        for m, c in combos[i].items():
            h = h + c * last[m]
        hess[(i, KRYLOV)] = h
    zero = jnp.zeros_like(gram[(1, 1)])
    unit = [zero + 1.0] + [zero] * (KRYLOV - 1)
    coeffs = [u / float(math.factorial(TAYLOR + 1)) for u in unit]
    for k in range(TAYLOR - 1, -1, -1):
        fresh = []
        for i in range(1, KRYLOV + 1):
            value = unit[i - 1] / float(math.factorial(k + 1))
            for j in range(max(i - 1, 1), KRYLOV + 1):
                value = value + step_size * hess[(i, j)] * coeffs[j - 1]
            fresh.append(value)
        coeffs = fresh
    out = p_ref[...]
    for m in range(1, KRYLOV + 1):
        factor = 0.0
        for i in range(m, KRYLOV + 1):
            factor = factor + coeffs[i - 1] * combos[i][m]
        out = out + step_size * hess[(1, 0)] * factor * q_ref[m - 1]
    out_ref[...] = out


def body(rate_terms, populations, temp_bins, bin_coeffs):
    core = lax.axis_index("k")
    n_bins = bin_coeffs.shape[0]
    cells = populations.shape[1]
    exchange = lambda v, axes: lax.all_to_all(v, axes, 0, 0, tiled=True)

    halves = rate_terms.reshape(TERMS, 2, NK, HALF, COLS)
    got = lax.ppermute(give_away(halves), "k", SWAP)
    got = pltpu.with_memory_space_constraint(got, pltpu.VMEM)
    kept = pltpu.with_memory_space_constraint(halves, pltpu.VMEM)

    onehot = (temp_bins[:, None] == jnp.arange(n_bins, dtype=jnp.int32)[None, :]).astype(
        jnp.float32
    )
    weights = jnp.dot(onehot, bin_coeffs, precision=lax.Precision.HIGHEST)
    weights = jnp.pad(weights.T, ((0, 2), (0, 0)))
    at = jnp.stack([core, lax.axis_index("z"), lax.axis_index("y") // 2]).astype(jnp.int32)

    def spread(piece):
        both = jnp.stack([piece, lax.ppermute(piece, "k", SWAP)])
        own = jnp.stack([lax.ppermute(both, ("z", "k", "x"), pairs) for pairs in SPREAD])
        other = lax.ppermute(own, "k", SWAP)
        return own.astype(jnp.float32), other.astype(jnp.float32)

    def reduce(partial):
        return exchange(partial.astype(WIRE), ("x", "y")).astype(jnp.float32)

    piece = populations.astype(jnp.bfloat16)
    own = jnp.stack([lax.ppermute(piece, ALL, pairs) for pairs in FIRST])
    first = own, lax.ppermute(own, "k", SWAP)
    met = reduce(apply_rates(at, kept, got, weights, [first], True))
    gram = jnp.zeros((16, cells), jnp.float32)
    q, gram = combine(0, met, gram, [])
    pieces, fields = [q], []
    for j in range(1, KRYLOV + 1):
        fields.append(spread(q.astype(WIRE)))
        if j == KRYLOV:
            outer = lax.ppermute(jnp.stack(pieces), ALL, TO_OUTER)
            fields[-1], outer = lax.optimization_barrier((fields[-1], outer))
        met = reduce(apply_rates(at, kept, got, weights, fields, False))
        if j < KRYLOV:
            q, gram = combine(j, met, gram, pieces)
            pieces.append(q)
        else:
            dots, gram = combine(j, met, gram, pieces)
    dots = dots + lax.ppermute(dots, "k", SWAP)
    dots = exchange(jnp.broadcast_to(dots[None], (NZ * NX * NY, *dots.shape)), ("z", "x", "y"))
    out = jax.ShapeDtypeStruct(populations.shape, jnp.float32)
    return call(finish_kernel, "finish", out, populations, outer, gram, dots)


def solution(mesh):
    named = Mesh(mesh.devices.reshape(NZ, NK, NX, NY), ALL)
    placed = (P(None, ("z", "k"), ("x", "y")), P(ALL, None), P(), P())
    return jax.shard_map(
        body, mesh=named, in_specs=placed, out_specs=P(ALL, None), check_vma=False
    )
```

```python
import math

import jax
import jax.numpy as jnp
from jax import lax
from jax.experimental import pallas as pl
from jax.experimental.pallas import tpu as pltpu
from jax.sharding import Mesh, PartitionSpec as P


KRYLOV = 4
TAYLOR = 8
TERMS = 6

epsilon = 1e-06
step_size = 1.0

NZ, NK, NX, NY = 4, 2, 4, 4
ALL = ("z", "k", "x", "y")
SUB = 64
HALF = NX * SUB
COLS = NK * HALF
WIRE = jnp.float16


def device(z, k, x, y):
    return ((z * NK + k) * NX + x) * NY + y


TO_INNER = [
    (device(z, k, x, y), device(z, (k + x) % 2, y, 2 * k + x // 2))
    for z in range(NZ)
    for k in range(NK)
    for x in range(NX)
    for y in range(NY)
]
TO_OUTER = [(b, a) for a, b in TO_INNER]
SWAP = [(0, 1), (1, 0)]
SPREAD = [
    [
        ((z * NK + k) * NX + x, (((x + 2 * k + t) % NZ) * NK + k) * NX + z)
        for z in range(NZ)
        for k in range(NK)
        for x in range(NX)
    ]
    for t in range(2)
]


def exponent(value):
    return jnp.floor(jnp.log2(jnp.maximum(jnp.abs(value), 1e-30)))


def solve(gram, count):
    g = lambda m, n: gram[(min(m, n), max(m, n))]
    scale = jnp.sqrt(g(1, 1) + epsilon)
    combos = {1: {1: 1.0 / scale}}
    hess = {(1, 0): scale}
    for j in range(1, count):
        d = {j + 1: None}
        for m in range(1, j + 1):
            d[m] = 0.0
        for i in range(1, j + 1):
            h = 0.0
            for m, c in combos[i].items():
                h = h + c * g(m, j + 1)
            hess[(i, j)] = h
            for m, c in combos[i].items():
                d[m] = d[m] - h * c
        square = g(j + 1, j + 1)
        for m in range(1, j + 1):
            inner = 2.0 * g(m, j + 1)
            for n in range(1, j + 1):
                inner = inner + d[n] * g(m, n)
            square = square + d[m] * inner
        length = jnp.sqrt(jnp.maximum(square, 0.0) + epsilon)
        hess[(j + 1, j)] = length
        inv = 1.0 / length
        combos[j + 1] = {m: (inv if m == j + 1 else d[m] * inv) for m in d}
    return combos, hess


def call(kernel, outs, *operands, scratch=(), far=(), limit=16):
    vmem = pl.BlockSpec(memory_space=pltpu.VMEM)
    specs = [
        pl.BlockSpec(memory_space=pltpu.SMEM) if a.dtype == jnp.int32 else vmem for a in operands
    ]
    for i in far:
        specs[i] = pl.BlockSpec(memory_space=pl.ANY)
    return pl.pallas_call(
        kernel,
        out_shape=outs,
        in_specs=specs,
        out_specs=jax.tree.map(lambda _: vmem, outs),
        scratch_shapes=scratch,
        compiler_params=pltpu.CompilerParams(vmem_limit_bytes=limit << 20),
    )(*operands)


def away_kernel(rates_ref, out_ref):
    out_ref[0] = rates_ref[0, :, 0]


def give_away(halves):
    return pl.pallas_call(
        away_kernel,
        out_shape=jax.ShapeDtypeStruct((TERMS, 2, HALF, COLS), halves.dtype),
        grid=(TERMS,),
        in_specs=[pl.BlockSpec((1, 2, 1, HALF, COLS), lambda g: (g, 0, 1, 0, 0))],
        out_specs=pl.BlockSpec((1, 2, HALF, COLS), lambda g: (g, 0, 0, 0)),
        compiler_params=pltpu.CompilerParams(vmem_limit_bytes=56 << 20),
        name="away",
    )(halves)


def extras(n_fields):
    return (1 + 3 * n_fields + 7) // 8 * 8


def matmul_kernel(n_fields, exact, at_ref, kept_ref, got_ref, w_ref, *refs):
    own_refs, other_refs = refs[:n_fields], refs[n_fields : 2 * n_fields]
    out_ref, x_ref = refs[2 * n_fields :][:2]
    core, place, side = at_ref[0], at_ref[1], at_ref[2]
    cells = w_ref.shape[1]
    copies = []
    if exact:
        held_ref, sems = refs[-2:]
        for h in range(2):
            copies.append(
                pltpu.make_async_copy(kept_ref.at[:, h, 0], held_ref.at[:, h], sems.at[h])
            )
            copies[h].start()

    for ref, k in ((own_refs[-1], core), (other_refs[-1], 1 - core)):
        for i in range(NX):
            t, o = divmod(i, 2)
            x, half = (place + 2 * NZ - 2 * k - t) % NX, (k + o + side) % 2
            value = ref[t, o]
            rows = pl.ds(pl.multiple_of(half * HALF + x * SUB, SUB), SUB)
            high = value.astype(jnp.bfloat16)
            x_ref[rows, pl.ds(0, cells)] = high
            if not exact:
                low = (value - high.astype(jnp.float32)).astype(jnp.bfloat16)
                x_ref[rows, pl.ds(cells, cells)] = low
    if not exact:
        extra_ref = refs[-1]
        extra_ref[...] = jnp.zeros_like(extra_ref)
        for m in range(n_fields):
            total = jnp.zeros((8, cells), jnp.float32)
            for a_ref, b_ref in ((own_refs[m], own_refs[-1]), (other_refs[m], other_refs[-1])):
                product = a_ref[...] * b_ref[...]
                total = total + jnp.sum(product.reshape(HALF // 8, 8, cells), axis=0)
            total = jnp.sum(total, axis=0, keepdims=True)
            power = exponent(total)
            total = total * jnp.exp2(-power)
            high = total.astype(jnp.bfloat16).astype(jnp.float32)
            extra_ref[pl.ds(3 * m + 1, 1), :] = power
            extra_ref[pl.ds(3 * m + 2, 1), :] = high
            extra_ref[pl.ds(3 * m + 3, 1), :] = (total - high) * 256.0

    for g in (2, 3, 0, 1):
        y = (g + 2 * core) % NY
        total = None
        if exact and g < 2:
            copies[g].wait()
        for j in range(TERMS):
            if g >= 2:
                rates = got_ref[j, g - 2]
            else:
                rates = held_ref[j, g] if exact else kept_ref[j, g, 0]
            product = jnp.dot(rates, x_ref[...], preferred_element_type=jnp.float32)
            if not exact:
                product = product[:, :cells] + product[:, cells:]
            product = w_ref[pl.ds(j, 1), :] * product
            total = product if total is None else total + product
        for x in range(NX):
            block = total[x * SUB : (x + 1) * SUB, :]
            if exact:
                out_ref[x, y] = block
                continue
            power = exponent(jnp.max(jnp.abs(block), axis=0, keepdims=True))
            out_ref[x, y, pl.ds(0, SUB), :] = block * jnp.exp2(-power)
            out_ref[x, y, pl.ds(SUB, extra_ref.shape[0]), :] = extra_ref[...]
            out_ref[x, y, pl.ds(SUB, 1), :] = power


def apply_rates(at, kept, got, weights, fields, exact):
    cells = weights.shape[1]
    more = 0 if exact else extras(len(fields))
    rows = SUB + more
    own, other = [f[0] for f in fields], [f[1] for f in fields]
    if exact:
        held = pltpu.VMEM((TERMS, 2, HALF, COLS), kept.dtype)
        last = [held, pltpu.SemaphoreType.DMA((2,))]
    else:
        last = [pltpu.VMEM((more, cells), jnp.float32)]

    def kernel(*refs):
        matmul_kernel(len(fields), exact, *refs)

    out = call(
        kernel,
        jax.ShapeDtypeStruct((NX, NY, rows, cells), jnp.float32),
        at,
        kept,
        got,
        weights,
        *own,
        *other,
        scratch=[pltpu.VMEM((COLS, cells if exact else 2 * cells), jnp.bfloat16)] + last,
        far=(1,) if exact else (),
        limit=46 if exact else 16,
    )
    return out.reshape(NX * NY, rows, cells)


def combine_kernel(j, got_ref, gram_ref, *refs):
    q_refs, outs = refs[:j], refs[j:]
    fresh, inner = None, [None] * j
    for b in range(NX * NY):
        value = got_ref[b, pl.ds(0, SUB), :]
        if j > 0:
            extra = got_ref[b, pl.ds(SUB, extras(j)), :]
            value = value * jnp.exp2(extra[:1])
        fresh = value if fresh is None else fresh + value
        for m in range(j):
            value = extra[3 * m + 2 : 3 * m + 3] + extra[3 * m + 3 : 3 * m + 4] * (1.0 / 256.0)
            value = value * jnp.exp2(extra[3 * m + 1 : 3 * m + 2])
            inner[m] = value if inner[m] is None else inner[m] + value
    gram_out = outs[-1]
    gram = {}
    if j > 0:
        gram_out[...] = gram_ref[...]
        for m in range(1, j + 1):
            for n in range(m, j):
                gram[(m, n)] = gram_ref[pl.ds(4 * (m - 1) + n - 1, 1), :]
            row = inner[m - 1]
            gram[(m, j)] = row
            gram_out[pl.ds(4 * (m - 1) + j - 1, 1), :] = row
        _, hess = solve(gram, j)
        for i in range(1, j):
            fresh = fresh - hess[(i, j - 1)] * q_refs[i][...]
        fresh = fresh * (1.0 / hess[(j, j - 1)])
    else:
        gram_out[...] = jnp.zeros_like(gram_out)
    if j < KRYLOV:
        outs[0][...] = fresh
    else:
        dots = outs[0]
        lanes = dots.shape[1]
        for m in range(1, KRYLOV + 1):
            row = jnp.sum(q_refs[m - 1][...] * fresh, axis=0, keepdims=True)
            dots[pl.ds(m - 1, 1), :] = row[:, :lanes]
            dots[pl.ds(KRYLOV + m - 1, 1), :] = row[:, lanes:]


def combine(j, got, gram, fields):
    cells = got.shape[2]

    def kernel(*refs):
        combine_kernel(j, *refs)

    if j < KRYLOV:
        outs = (jax.ShapeDtypeStruct((SUB, cells), jnp.float32),)
    else:
        outs = (jax.ShapeDtypeStruct((2 * KRYLOV, cells // 2), jnp.float32),)
    outs = (*outs, jax.ShapeDtypeStruct(gram.shape, jnp.float32))
    return call(kernel, outs, got, gram, *fields)


def finish_kernel(p_ref, q_ref, gram_ref, dots_ref, out_ref):
    gram = {}
    for m in range(1, KRYLOV + 1):
        for n in range(m, KRYLOV + 1):
            gram[(m, n)] = gram_ref[pl.ds(4 * (m - 1) + n - 1, 1), :]
    dots = jnp.sum(dots_ref[...], axis=0)
    last = {
        m: jnp.concatenate([dots[m - 1 : m], dots[KRYLOV + m - 1 : KRYLOV + m]], axis=1)
        for m in range(1, KRYLOV + 1)
    }
    combos, hess = solve(gram, KRYLOV)
    for i in range(1, KRYLOV + 1):
        h = 0.0
        for m, c in combos[i].items():
            h = h + c * last[m]
        hess[(i, KRYLOV)] = h
    zero = jnp.zeros_like(gram[(1, 1)])
    unit = [zero + 1.0] + [zero] * (KRYLOV - 1)
    coeffs = [u / float(math.factorial(TAYLOR + 1)) for u in unit]
    for k in range(TAYLOR - 1, -1, -1):
        fresh = []
        for i in range(1, KRYLOV + 1):
            value = unit[i - 1] / float(math.factorial(k + 1))
            for j in range(max(i - 1, 1), KRYLOV + 1):
                value = value + step_size * hess[(i, j)] * coeffs[j - 1]
            fresh.append(value)
        coeffs = fresh
    out = p_ref[...]
    for m in range(1, KRYLOV + 1):
        factor = 0.0
        for i in range(m, KRYLOV + 1):
            factor = factor + coeffs[i - 1] * combos[i][m]
        out = out + step_size * hess[(1, 0)] * factor * q_ref[m - 1]
    out_ref[...] = out


def body(rate_terms, populations, temp_bins, bin_coeffs):
    core = lax.axis_index("k")
    n_bins = bin_coeffs.shape[0]
    cells = populations.shape[1]
    exchange = lambda v, axes: lax.all_to_all(v, axes, 0, 0, tiled=True)

    halves = rate_terms.reshape(TERMS, 2, NK, HALF, COLS)
    away = give_away(halves)
    got = lax.ppermute(away, "k", SWAP)
    got = pltpu.with_memory_space_constraint(got, pltpu.VMEM)
    kept = pltpu.with_memory_space_constraint(halves, pltpu.VMEM)

    onehot = (temp_bins[:, None] == jnp.arange(n_bins, dtype=jnp.int32)[None, :]).astype(
        jnp.float32
    )
    weights = jnp.dot(onehot, bin_coeffs, precision=lax.Precision.HIGHEST)
    weights = jnp.pad(weights.T, ((0, 2), (0, 0)))
    at = jnp.stack([core, lax.axis_index("z"), lax.axis_index("y") // 2]).astype(jnp.int32)

    def spread(piece):
        wide = jnp.float32 if piece.dtype == WIRE else piece.dtype
        both = jnp.stack([piece, lax.ppermute(piece, "k", SWAP)])
        own = jnp.stack([lax.ppermute(both, ("z", "k", "x"), pairs) for pairs in SPREAD])
        other = lax.ppermute(own, "k", SWAP)
        return own.astype(wide), other.astype(wide)

    def reduce(partial):
        return exchange(partial.astype(WIRE), ("x", "y")).astype(jnp.float32)

    piece = lax.ppermute(populations.astype(jnp.bfloat16), ALL, TO_INNER)
    first = spread(piece)
    met = reduce(apply_rates(at, halves, got, weights, [first], True))
    gram = jnp.zeros((16, cells), jnp.float32)
    q, gram = combine(0, met, gram, [])
    pieces, fields = [q], []
    for j in range(1, KRYLOV + 1):
        fields.append(spread(q.astype(WIRE)))
        if j == KRYLOV:
            outer = lax.ppermute(jnp.stack(pieces), ALL, TO_OUTER)
        partial = apply_rates(at, kept, got, weights, fields, False)
        met = reduce(partial)
        if j < KRYLOV:
            q, gram = combine(j, met, gram, pieces)
            pieces.append(q)
        else:
            dots, gram = combine(j, met, gram, pieces)
    dots = dots + lax.ppermute(dots, "k", SWAP)
    dots = exchange(jnp.broadcast_to(dots[None], (NZ * NX * NY, *dots.shape)), ("z", "x", "y"))
    out = jax.ShapeDtypeStruct(populations.shape, jnp.float32)
    return call(finish_kernel, out, populations, outer, gram, dots)


def solution(mesh):
    named = Mesh(mesh.devices.reshape(NZ, NK, NX, NY), ALL)
    placed = (P(None, ("z", "k"), ("x", "y")), P(ALL, None), P(), P())
    return jax.shard_map(body, mesh=named, in_specs=placed, out_specs=P(ALL, None), check_vma=False)
```

```python
import math

import jax
import jax.numpy as jnp
from jax import lax
from jax.experimental import pallas as pl
from jax.experimental.pallas import tpu as pltpu
from jax.sharding import Mesh, PartitionSpec as P


KRYLOV = 4
TAYLOR = 8
TERMS = 6

epsilon = 1e-06
step_size = 1.0

NZ, NK, NX, NY = 4, 2, 4, 4
ALL = ("z", "k", "x", "y")
SUB = 64
HALF = NX * SUB
COLS = NK * HALF
WIRE = jnp.float16


def device(z, k, x, y):
    return ((z * NK + k) * NX + x) * NY + y


TO_INNER = [
    (device(z, k, x, y), device(z, (k + x) % 2, y, 2 * k + x // 2))
    for z in range(NZ)
    for k in range(NK)
    for x in range(NX)
    for y in range(NY)
]
TO_OUTER = [(b, a) for a, b in TO_INNER]
SWAP = [(0, 1), (1, 0)]
SPREAD = [
    [
        ((z * NK + k) * NX + x, (((x + 2 * k + t) % NZ) * NK + k) * NX + z)
        for z in range(NZ)
        for k in range(NK)
        for x in range(NX)
    ]
    for t in range(2)
]


def exponent(value):
    return jnp.floor(jnp.log2(jnp.maximum(jnp.abs(value), 1e-30)))


def solve(gram, count):
    g = lambda m, n: gram[(min(m, n), max(m, n))]
    scale = jnp.sqrt(g(1, 1) + epsilon)
    combos = {1: {1: 1.0 / scale}}
    hess = {(1, 0): scale}
    for j in range(1, count):
        d = {j + 1: None}
        for m in range(1, j + 1):
            d[m] = 0.0
        for i in range(1, j + 1):
            h = 0.0
            for m, c in combos[i].items():
                h = h + c * g(m, j + 1)
            hess[(i, j)] = h
            for m, c in combos[i].items():
                d[m] = d[m] - h * c
        square = g(j + 1, j + 1)
        for m in range(1, j + 1):
            inner = 2.0 * g(m, j + 1)
            for n in range(1, j + 1):
                inner = inner + d[n] * g(m, n)
            square = square + d[m] * inner
        length = jnp.sqrt(jnp.maximum(square, 0.0) + epsilon)
        hess[(j + 1, j)] = length
        inv = 1.0 / length
        combos[j + 1] = {m: (inv if m == j + 1 else d[m] * inv) for m in d}
    return combos, hess


def call(kernel, outs, *operands, scratch=(), far=(), limit=16):
    vmem = pl.BlockSpec(memory_space=pltpu.VMEM)
    specs = [
        pl.BlockSpec(memory_space=pltpu.SMEM) if a.dtype == jnp.int32 else vmem for a in operands
    ]
    for i in far:
        specs[i] = pl.BlockSpec(memory_space=pl.ANY)
    return pl.pallas_call(
        kernel,
        out_shape=outs,
        in_specs=specs,
        out_specs=jax.tree.map(lambda _: vmem, outs),
        scratch_shapes=scratch,
        compiler_params=pltpu.CompilerParams(vmem_limit_bytes=limit << 20),
    )(*operands)


def extras(n_fields):
    return (1 + 3 * n_fields + 7) // 8 * 8


def matmul_kernel(n_fields, exact, at_ref, kept_ref, got_ref, w_ref, *refs):
    own_refs, other_refs = refs[:n_fields], refs[n_fields : 2 * n_fields]
    out_ref, x_ref = refs[2 * n_fields :][:2]
    core, place, side = at_ref[0], at_ref[1], at_ref[2]
    cells = w_ref.shape[1]
    copies = []
    if exact:
        held_ref, sems = refs[-2:]
        for h in range(2):
            copies.append(
                pltpu.make_async_copy(kept_ref.at[:, h, 0], held_ref.at[:, h], sems.at[h])
            )
            copies[h].start()

    for ref, k in ((own_refs[-1], core), (other_refs[-1], 1 - core)):
        for i in range(NX):
            t, o = divmod(i, 2)
            x, half = (place + 2 * NZ - 2 * k - t) % NX, (k + o + side) % 2
            value = ref[t, o]
            rows = pl.ds(pl.multiple_of(half * HALF + x * SUB, SUB), SUB)
            high = value.astype(jnp.bfloat16)
            x_ref[rows, pl.ds(0, cells)] = high
            if not exact:
                low = (value - high.astype(jnp.float32)).astype(jnp.bfloat16)
                x_ref[rows, pl.ds(cells, cells)] = low
    if not exact:
        extra_ref = refs[-1]
        extra_ref[...] = jnp.zeros_like(extra_ref)
        for m in range(n_fields):
            total = jnp.zeros((8, cells), jnp.float32)
            for a_ref, b_ref in ((own_refs[m], own_refs[-1]), (other_refs[m], other_refs[-1])):
                product = a_ref[...] * b_ref[...]
                total = total + jnp.sum(product.reshape(HALF // 8, 8, cells), axis=0)
            total = jnp.sum(total, axis=0, keepdims=True)
            power = exponent(total)
            total = total * jnp.exp2(-power)
            high = total.astype(jnp.bfloat16).astype(jnp.float32)
            extra_ref[pl.ds(3 * m + 1, 1), :] = power
            extra_ref[pl.ds(3 * m + 2, 1), :] = high
            extra_ref[pl.ds(3 * m + 3, 1), :] = (total - high) * 256.0

    for g in (2, 3, 0, 1):
        y = (g + 2 * core) % NY
        total = None
        if exact and g < 2:
            copies[g].wait()
        for j in range(TERMS):
            if g >= 2:
                rates = got_ref[j, g - 2]
            else:
                rates = held_ref[j, g] if exact else kept_ref[j, g, 0]
            product = jnp.dot(rates, x_ref[...], preferred_element_type=jnp.float32)
            if not exact:
                product = product[:, :cells] + product[:, cells:]
            product = w_ref[pl.ds(j, 1), :] * product
            total = product if total is None else total + product
        for x in range(NX):
            block = total[x * SUB : (x + 1) * SUB, :]
            if exact:
                out_ref[x, y] = block
                continue
            power = exponent(jnp.max(jnp.abs(block), axis=0, keepdims=True))
            out_ref[x, y, pl.ds(0, SUB), :] = block * jnp.exp2(-power)
            out_ref[x, y, pl.ds(SUB, extra_ref.shape[0]), :] = extra_ref[...]
            out_ref[x, y, pl.ds(SUB, 1), :] = power


def apply_rates(at, kept, got, weights, fields, exact):
    cells = weights.shape[1]
    more = 0 if exact else extras(len(fields))
    rows = SUB + more
    own, other = [f[0] for f in fields], [f[1] for f in fields]
    if exact:
        held = pltpu.VMEM((TERMS, 2, HALF, COLS), kept.dtype)
        last = [held, pltpu.SemaphoreType.DMA((2,))]
    else:
        last = [pltpu.VMEM((more, cells), jnp.float32)]

    def kernel(*refs):
        matmul_kernel(len(fields), exact, *refs)

    out = call(
        kernel,
        jax.ShapeDtypeStruct((NX, NY, rows, cells), jnp.float32),
        at,
        kept,
        got,
        weights,
        *own,
        *other,
        scratch=[pltpu.VMEM((COLS, cells if exact else 2 * cells), jnp.bfloat16)] + last,
        far=(1,) if exact else (),
        limit=46 if exact else 16,
    )
    return out.reshape(NX * NY, rows, cells)


def combine_kernel(j, got_ref, gram_ref, *refs):
    q_refs, outs = refs[:j], refs[j:]
    fresh, inner = None, [None] * j
    for b in range(NX * NY):
        value = got_ref[b, pl.ds(0, SUB), :]
        if j > 0:
            extra = got_ref[b, pl.ds(SUB, extras(j)), :]
            value = value * jnp.exp2(extra[:1])
        fresh = value if fresh is None else fresh + value
        for m in range(j):
            value = extra[3 * m + 2 : 3 * m + 3] + extra[3 * m + 3 : 3 * m + 4] * (1.0 / 256.0)
            value = value * jnp.exp2(extra[3 * m + 1 : 3 * m + 2])
            inner[m] = value if inner[m] is None else inner[m] + value
    gram_out = outs[-1]
    gram = {}
    if j > 0:
        gram_out[...] = gram_ref[...]
        for m in range(1, j + 1):
            for n in range(m, j):
                gram[(m, n)] = gram_ref[pl.ds(4 * (m - 1) + n - 1, 1), :]
            row = inner[m - 1]
            gram[(m, j)] = row
            gram_out[pl.ds(4 * (m - 1) + j - 1, 1), :] = row
        _, hess = solve(gram, j)
        for i in range(1, j):
            fresh = fresh - hess[(i, j - 1)] * q_refs[i][...]
        fresh = fresh * (1.0 / hess[(j, j - 1)])
    else:
        gram_out[...] = jnp.zeros_like(gram_out)
    if j < KRYLOV:
        outs[0][...] = fresh
    else:
        dots = outs[0]
        lanes = dots.shape[1]
        for m in range(1, KRYLOV + 1):
            row = jnp.sum(q_refs[m - 1][...] * fresh, axis=0, keepdims=True)
            dots[pl.ds(m - 1, 1), :] = row[:, :lanes]
            dots[pl.ds(KRYLOV + m - 1, 1), :] = row[:, lanes:]


def combine(j, got, gram, fields):
    cells = got.shape[2]

    def kernel(*refs):
        combine_kernel(j, *refs)

    if j < KRYLOV:
        outs = (jax.ShapeDtypeStruct((SUB, cells), jnp.float32),)
    else:
        outs = (jax.ShapeDtypeStruct((2 * KRYLOV, cells // 2), jnp.float32),)
    outs = (*outs, jax.ShapeDtypeStruct(gram.shape, jnp.float32))
    return call(kernel, outs, got, gram, *fields)


def pair_kernel(mine_ref, other_ref, out_ref):
    out_ref[...] = jnp.broadcast_to((mine_ref[...] + other_ref[...])[None], out_ref.shape)


def finish_kernel(p_ref, q_ref, gram_ref, dots_ref, out_ref):
    gram = {}
    for m in range(1, KRYLOV + 1):
        for n in range(m, KRYLOV + 1):
            gram[(m, n)] = gram_ref[pl.ds(4 * (m - 1) + n - 1, 1), :]
    dots = jnp.sum(dots_ref[...], axis=0)
    last = {
        m: jnp.concatenate([dots[m - 1 : m], dots[KRYLOV + m - 1 : KRYLOV + m]], axis=1)
        for m in range(1, KRYLOV + 1)
    }
    combos, hess = solve(gram, KRYLOV)
    for i in range(1, KRYLOV + 1):
        h = 0.0
        for m, c in combos[i].items():
            h = h + c * last[m]
        hess[(i, KRYLOV)] = h
    zero = jnp.zeros_like(gram[(1, 1)])
    unit = [zero + 1.0] + [zero] * (KRYLOV - 1)
    coeffs = [u / float(math.factorial(TAYLOR + 1)) for u in unit]
    for k in range(TAYLOR - 1, -1, -1):
        fresh = []
        for i in range(1, KRYLOV + 1):
            value = unit[i - 1] / float(math.factorial(k + 1))
            for j in range(max(i - 1, 1), KRYLOV + 1):
                value = value + step_size * hess[(i, j)] * coeffs[j - 1]
            fresh.append(value)
        coeffs = fresh
    out = p_ref[...]
    for m in range(1, KRYLOV + 1):
        factor = 0.0
        for i in range(m, KRYLOV + 1):
            factor = factor + coeffs[i - 1] * combos[i][m]
        out = out + step_size * hess[(1, 0)] * factor * q_ref[m - 1]
    out_ref[...] = out


def body(rate_terms, populations, temp_bins, bin_coeffs):
    core = lax.axis_index("k")
    n_bins = bin_coeffs.shape[0]
    cells = populations.shape[1]
    exchange = lambda v, axes: lax.all_to_all(v, axes, 0, 0, tiled=True)

    halves = rate_terms.reshape(TERMS, 2, NK, HALF, COLS)
    away = halves[:, :, 1]
    kept = pltpu.with_memory_space_constraint(halves, pltpu.VMEM)

    onehot = (temp_bins[:, None] == jnp.arange(n_bins, dtype=jnp.int32)[None, :]).astype(
        jnp.float32
    )
    weights = jnp.dot(onehot, bin_coeffs, precision=lax.Precision.HIGHEST)
    weights = jnp.pad(weights.T, ((0, 2), (0, 0)))
    at = jnp.stack([core, lax.axis_index("z"), lax.axis_index("y") // 2]).astype(jnp.int32)

    def spread(both):
        wide = jnp.float32 if both.dtype == WIRE else both.dtype
        own = jnp.stack([lax.ppermute(both, ("z", "k", "x"), pairs) for pairs in SPREAD])
        other = lax.ppermute(own, "k", SWAP)
        return own.astype(wide), other.astype(wide)

    def reduce(partial):
        return exchange(partial.astype(WIRE), ("x", "y")).astype(jnp.float32)

    piece = lax.ppermute(populations.astype(jnp.bfloat16), ALL, TO_INNER)
    both = jnp.stack([piece, lax.ppermute(piece, "k", SWAP)])
    away, both = lax.optimization_barrier((away, both))
    got = lax.ppermute(away, "k", SWAP)
    got = pltpu.with_memory_space_constraint(got, pltpu.VMEM)
    first = spread(both)
    met = reduce(apply_rates(at, halves, got, weights, [first], True))
    gram = jnp.zeros((16, cells), jnp.float32)
    q, gram = combine(0, met, gram, [])
    pieces, fields = [q], []
    for j in range(1, KRYLOV + 1):
        piece = q.astype(WIRE)
        fields.append(spread(jnp.stack([piece, lax.ppermute(piece, "k", SWAP)])))
        if j == KRYLOV:
            outer = lax.ppermute(jnp.stack(pieces).astype(WIRE), ALL, TO_OUTER)
        partial = apply_rates(at, kept, got, weights, fields, False)
        met = reduce(partial)
        if j < KRYLOV:
            q, gram = combine(j, met, gram, pieces)
            pieces.append(q)
        else:
            dots, gram = combine(j, met, gram, pieces)
    dots = call(
        pair_kernel,
        jax.ShapeDtypeStruct((NZ * NX * NY, *dots.shape), dots.dtype),
        dots,
        lax.ppermute(dots, "k", SWAP),
    )
    dots = exchange(dots, ("z", "x", "y"))
    outer = outer.astype(jnp.float32)
    out = jax.ShapeDtypeStruct(populations.shape, jnp.float32)
    return call(finish_kernel, out, populations, outer, gram, dots)


def solution(mesh):
    named = Mesh(mesh.devices.reshape(NZ, NK, NX, NY), ALL)
    placed = (P(None, ("z", "k"), ("x", "y")), P(ALL, None), P(), P())
    return jax.shard_map(body, mesh=named, in_specs=placed, out_specs=P(ALL, None), check_vma=False)
```

```python
import math

import jax
import jax.numpy as jnp
from jax import lax
from jax.experimental import pallas as pl
from jax.experimental.pallas import tpu as pltpu
from jax.sharding import Mesh, PartitionSpec as P


KRYLOV = 4
TAYLOR = 8
TERMS = 6

epsilon = 1e-06
step_size = 1.0

NZ, NK, NX, NY = 4, 2, 4, 4
ALL = ("z", "k", "x", "y")
SUB = 64
HALF = NX * SUB
COLS = NK * HALF
WIRE = jnp.float16


def device(z, k, x, y):
    return ((z * NK + k) * NX + x) * NY + y


TO_INNER = [
    (device(z, k, x, y), device(z, (k + x) % 2, y, 2 * k + x // 2))
    for z in range(NZ)
    for k in range(NK)
    for x in range(NX)
    for y in range(NY)
]
TO_OUTER = [(b, a) for a, b in TO_INNER]
SWAP = [(0, 1), (1, 0)]
SPREAD = [
    [
        ((z * NK + k) * NX + x, (((x + 2 * k + t) % NZ) * NK + k) * NX + z)
        for z in range(NZ)
        for k in range(NK)
        for x in range(NX)
    ]
    for t in range(2)
]


def exponent(value):
    return jnp.floor(jnp.log2(jnp.maximum(jnp.abs(value), 1e-30)))


def solve(gram, count):
    g = lambda m, n: gram[(min(m, n), max(m, n))]
    scale = jnp.sqrt(g(1, 1) + epsilon)
    combos = {1: {1: 1.0 / scale}}
    hess = {(1, 0): scale}
    for j in range(1, count):
        d = {j + 1: None}
        for m in range(1, j + 1):
            d[m] = 0.0
        for i in range(1, j + 1):
            h = 0.0
            for m, c in combos[i].items():
                h = h + c * g(m, j + 1)
            hess[(i, j)] = h
            for m, c in combos[i].items():
                d[m] = d[m] - h * c
        square = g(j + 1, j + 1)
        for m in range(1, j + 1):
            inner = 2.0 * g(m, j + 1)
            for n in range(1, j + 1):
                inner = inner + d[n] * g(m, n)
            square = square + d[m] * inner
        length = jnp.sqrt(jnp.maximum(square, 1e-7 * g(j + 1, j + 1)) + epsilon)
        hess[(j + 1, j)] = length
        inv = 1.0 / length
        combos[j + 1] = {m: (inv if m == j + 1 else d[m] * inv) for m in d}
    return combos, hess


def call(kernel, outs, *operands, scratch=(), far=(), limit=16):
    vmem = pl.BlockSpec(memory_space=pltpu.VMEM)
    specs = [
        pl.BlockSpec(memory_space=pltpu.SMEM) if a.dtype == jnp.int32 else vmem for a in operands
    ]
    for i in far:
        specs[i] = pl.BlockSpec(memory_space=pl.ANY)
    return pl.pallas_call(
        kernel,
        out_shape=outs,
        in_specs=specs,
        out_specs=jax.tree.map(lambda _: vmem, outs),
        scratch_shapes=scratch,
        compiler_params=pltpu.CompilerParams(vmem_limit_bytes=limit << 20),
    )(*operands)


def extras(n_fields):
    return (1 + 3 * n_fields + 7) // 8 * 8


def matmul_kernel(n_fields, exact, at_ref, kept_ref, got_ref, w_ref, *refs):
    own_refs, other_refs = refs[:n_fields], refs[n_fields : 2 * n_fields]
    out_ref, x_ref = refs[2 * n_fields :][:2]
    core, place, side = at_ref[0], at_ref[1], at_ref[2]
    cells = w_ref.shape[1]
    copies = []
    if exact:
        held_ref, sems = refs[-2:]
        for h in range(2):
            copies.append(
                pltpu.make_async_copy(kept_ref.at[:, h, 0], held_ref.at[:, h], sems.at[h])
            )
            copies[h].start()

    for ref, k in ((own_refs[-1], core), (other_refs[-1], 1 - core)):
        for i in range(NX):
            t, o = divmod(i, 2)
            x, half = (place + 2 * NZ - 2 * k - t) % NX, (k + o + side) % 2
            value = ref[t, o]
            rows = pl.ds(pl.multiple_of(half * HALF + x * SUB, SUB), SUB)
            high = value.astype(jnp.bfloat16)
            x_ref[rows, pl.ds(0, cells)] = high
            if not exact:
                low = (value - high.astype(jnp.float32)).astype(jnp.bfloat16)
                x_ref[rows, pl.ds(cells, cells)] = low
    if not exact:
        extra_ref = refs[-1]
        extra_ref[...] = jnp.zeros_like(extra_ref)
        for m in range(n_fields):
            total = jnp.zeros((8, cells), jnp.float32)
            for a_ref, b_ref in ((own_refs[m], own_refs[-1]), (other_refs[m], other_refs[-1])):
                product = a_ref[...] * b_ref[...]
                total = total + jnp.sum(product.reshape(HALF // 8, 8, cells), axis=0)
            total = jnp.sum(total, axis=0, keepdims=True)
            power = exponent(total)
            total = total * jnp.exp2(-power)
            high = total.astype(jnp.bfloat16).astype(jnp.float32)
            extra_ref[pl.ds(3 * m + 1, 1), :] = power
            extra_ref[pl.ds(3 * m + 2, 1), :] = high
            extra_ref[pl.ds(3 * m + 3, 1), :] = (total - high) * 256.0

    for g in (2, 3, 0, 1):
        y = (g + 2 * core) % NY
        total = None
        if exact and g < 2:
            copies[g].wait()
        for j in range(TERMS):
            if g >= 2:
                rates = got_ref[j, g - 2]
            else:
                rates = held_ref[j, g] if exact else kept_ref[j, g, 0]
            product = jnp.dot(rates, x_ref[...], preferred_element_type=jnp.float32)
            if not exact:
                product = product[:, :cells] + product[:, cells:]
            product = w_ref[pl.ds(j, 1), :] * product
            total = product if total is None else total + product
        for x in range(NX):
            block = total[x * SUB : (x + 1) * SUB, :]
            if exact:
                out_ref[x, y] = block
                continue
            power = exponent(jnp.max(jnp.abs(block), axis=0, keepdims=True))
            out_ref[x, y, pl.ds(0, SUB), :] = block * jnp.exp2(-power)
            out_ref[x, y, pl.ds(SUB, extra_ref.shape[0]), :] = extra_ref[...]
            out_ref[x, y, pl.ds(SUB, 1), :] = power


def apply_rates(at, kept, got, weights, fields, exact):
    cells = weights.shape[1]
    more = 0 if exact else extras(len(fields))
    rows = SUB + more
    own, other = [f[0] for f in fields], [f[1] for f in fields]
    if exact:
        held = pltpu.VMEM((TERMS, 2, HALF, COLS), kept.dtype)
        last = [held, pltpu.SemaphoreType.DMA((2,))]
    else:
        last = [pltpu.VMEM((more, cells), jnp.float32)]

    def kernel(*refs):
        matmul_kernel(len(fields), exact, *refs)

    out = call(
        kernel,
        jax.ShapeDtypeStruct((NX, NY, rows, cells), jnp.float32),
        at,
        kept,
        got,
        weights,
        *own,
        *other,
        scratch=[pltpu.VMEM((COLS, cells if exact else 2 * cells), jnp.bfloat16)] + last,
        far=(1,) if exact else (),
        limit=46 if exact else 16,
    )
    return out.reshape(NX * NY, rows, cells)


def combine_kernel(j, got_ref, gram_ref, *refs):
    q_refs, outs = refs[:j], refs[j:]
    fresh, inner = None, [None] * j
    for b in range(NX * NY):
        value = got_ref[b, pl.ds(0, SUB), :]
        if j > 0:
            extra = got_ref[b, pl.ds(SUB, extras(j)), :]
            value = value * jnp.exp2(extra[:1])
        fresh = value if fresh is None else fresh + value
        for m in range(j):
            value = extra[3 * m + 2 : 3 * m + 3] + extra[3 * m + 3 : 3 * m + 4] * (1.0 / 256.0)
            value = value * jnp.exp2(extra[3 * m + 1 : 3 * m + 2])
            inner[m] = value if inner[m] is None else inner[m] + value
    gram_out = outs[-1]
    gram = {}
    if j > 0:
        gram_out[...] = gram_ref[...]
        for m in range(1, j + 1):
            for n in range(m, j):
                gram[(m, n)] = gram_ref[pl.ds(4 * (m - 1) + n - 1, 1), :]
            row = inner[m - 1]
            gram[(m, j)] = row
            gram_out[pl.ds(4 * (m - 1) + j - 1, 1), :] = row
        _, hess = solve(gram, j)
        for i in range(1, j):
            fresh = fresh - hess[(i, j - 1)] * q_refs[i][...]
        fresh = fresh * (1.0 / hess[(j, j - 1)])
    else:
        gram_out[...] = jnp.zeros_like(gram_out)
    if j < KRYLOV:
        outs[0][...] = fresh
    else:
        dots = outs[0]
        lanes = dots.shape[1]
        for m in range(1, KRYLOV + 1):
            row = jnp.sum(q_refs[m - 1][...] * fresh, axis=0, keepdims=True)
            dots[pl.ds(m - 1, 1), :] = row[:, :lanes]
            dots[pl.ds(KRYLOV + m - 1, 1), :] = row[:, lanes:]


def combine(j, got, gram, fields):
    cells = got.shape[2]

    def kernel(*refs):
        combine_kernel(j, *refs)

    if j < KRYLOV:
        outs = (jax.ShapeDtypeStruct((SUB, cells), jnp.float32),)
    else:
        outs = (jax.ShapeDtypeStruct((2 * KRYLOV, cells // 2), jnp.float32),)
    outs = (*outs, jax.ShapeDtypeStruct(gram.shape, jnp.float32))
    return call(kernel, outs, got, gram, *fields)


def pair_kernel(mine_ref, other_ref, out_ref):
    out_ref[...] = jnp.broadcast_to((mine_ref[...] + other_ref[...])[None], out_ref.shape)


def finish_kernel(p_ref, q_ref, gram_ref, dots_ref, out_ref):
    gram = {}
    for m in range(1, KRYLOV + 1):
        for n in range(m, KRYLOV + 1):
            gram[(m, n)] = gram_ref[pl.ds(4 * (m - 1) + n - 1, 1), :]
    dots = jnp.sum(dots_ref[...], axis=0)
    last = {
        m: jnp.concatenate([dots[m - 1 : m], dots[KRYLOV + m - 1 : KRYLOV + m]], axis=1)
        for m in range(1, KRYLOV + 1)
    }
    combos, hess = solve(gram, KRYLOV)
    for i in range(1, KRYLOV + 1):
        h = 0.0
        for m, c in combos[i].items():
            h = h + c * last[m]
        hess[(i, KRYLOV)] = h
    zero = jnp.zeros_like(gram[(1, 1)])
    unit = [zero + 1.0] + [zero] * (KRYLOV - 1)
    coeffs = [u / float(math.factorial(TAYLOR + 1)) for u in unit]
    for k in range(TAYLOR - 1, -1, -1):
        fresh = []
        for i in range(1, KRYLOV + 1):
            value = unit[i - 1] / float(math.factorial(k + 1))
            for j in range(max(i - 1, 1), KRYLOV + 1):
                value = value + step_size * hess[(i, j)] * coeffs[j - 1]
            fresh.append(value)
        coeffs = fresh
    out = p_ref[...]
    for m in range(1, KRYLOV + 1):
        factor = 0.0
        for i in range(m, KRYLOV + 1):
            factor = factor + coeffs[i - 1] * combos[i][m]
        out = out + step_size * hess[(1, 0)] * factor * q_ref[m - 1]
    out_ref[...] = out


def body(rate_terms, populations, temp_bins, bin_coeffs):
    core = lax.axis_index("k")
    n_bins = bin_coeffs.shape[0]
    cells = populations.shape[1]
    exchange = lambda v, axes: lax.all_to_all(v, axes, 0, 0, tiled=True)

    halves = rate_terms.reshape(TERMS, 2, NK, HALF, COLS)
    away = halves[:, :, 1]
    kept = pltpu.with_memory_space_constraint(halves, pltpu.VMEM)

    onehot = (temp_bins[:, None] == jnp.arange(n_bins, dtype=jnp.int32)[None, :]).astype(
        jnp.float32
    )
    weights = jnp.dot(onehot, bin_coeffs, precision=lax.Precision.HIGHEST)
    weights = jnp.pad(weights.T, ((0, 2), (0, 0)))
    at = jnp.stack([core, lax.axis_index("z"), lax.axis_index("y") // 2]).astype(jnp.int32)

    def spread(both):
        wide = jnp.float32 if both.dtype == WIRE else both.dtype
        own = [lax.ppermute(both, ("z", "k", "x"), pairs) for pairs in SPREAD]
        own = jnp.stack(own)
        other = lax.ppermute(own, "k", SWAP)
        return own.astype(wide), other.astype(wide)

    def reduce(partial):
        return exchange(partial.astype(WIRE), ("x", "y")).astype(jnp.float32)

    piece = lax.ppermute(populations.astype(jnp.bfloat16), ALL, TO_INNER)
    both = jnp.stack([piece, lax.ppermute(piece, "k", SWAP)])
    away, both = lax.optimization_barrier((away, both))
    got = lax.ppermute(away, "k", SWAP)
    got = pltpu.with_memory_space_constraint(got, pltpu.VMEM)
    first = spread(both)
    met = reduce(apply_rates(at, halves, got, weights, [first], True))
    gram = jnp.zeros((16, cells), jnp.float32)
    q, gram = combine(0, met, gram, [])
    pieces, fields = [q], []
    for j in range(1, KRYLOV + 1):
        piece = q.astype(WIRE)
        both = jnp.stack([piece, lax.ppermute(piece, "k", SWAP)])
        fields.append(spread(both))
        if j == KRYLOV:
            outer = lax.ppermute(jnp.stack(pieces).astype(WIRE), ALL, TO_OUTER)
        partial = apply_rates(at, kept, got, weights, fields, False)
        met = reduce(partial)
        if j < KRYLOV:
            q, gram = combine(j, met, gram, pieces)
            pieces.append(q)
        else:
            dots, gram = combine(j, met, gram, pieces)
    dots = call(
        pair_kernel,
        jax.ShapeDtypeStruct((NZ * NX * NY, *dots.shape), dots.dtype),
        dots,
        lax.ppermute(dots, "k", SWAP),
    )
    dots, outer = lax.optimization_barrier((dots, outer.astype(jnp.float32)))
    dots = exchange(dots, ("z", "x", "y"))
    out = jax.ShapeDtypeStruct(populations.shape, jnp.float32)
    return call(finish_kernel, out, populations, outer, gram, dots)


def solution(mesh):
    named = Mesh(mesh.devices.reshape(NZ, NK, NX, NY), ALL)
    placed = (P(None, ("z", "k"), ("x", "y")), P(ALL, None), P(), P())
    return jax.shard_map(body, mesh=named, in_specs=placed, out_specs=P(ALL, None), check_vma=False)
```

```python
import math

import jax
import jax.numpy as jnp
from jax import lax
from jax.experimental import pallas as pl
from jax.experimental.pallas import tpu as pltpu
from jax.sharding import Mesh, PartitionSpec as P


KRYLOV = 4
TAYLOR = 8
TERMS = 6

epsilon = 1e-06
step_size = 1.0

NZ, NK, NX, NY = 4, 2, 4, 4
ALL = ("z", "k", "x", "y")
SUB = 64
HALF = NX * SUB
COLS = NK * HALF
WIRE = jnp.float16


def device(z, k, x, y):
    return ((z * NK + k) * NX + x) * NY + y


TO_INNER = [
    (device(z, k, x, y), device(z, (k + x) % 2, y, 2 * k + x // 2))
    for z in range(NZ)
    for k in range(NK)
    for x in range(NX)
    for y in range(NY)
]
TO_OUTER = [(b, a) for a, b in TO_INNER]
SWAP = [(0, 1), (1, 0)]
SPREAD = [
    [
        ((z * NK + k) * NX + x, (((x + 2 * k + t) % NZ) * NK + k) * NX + z)
        for z in range(NZ)
        for k in range(NK)
        for x in range(NX)
    ]
    for t in range(2)
]


def exponent(value):
    return jnp.floor(jnp.log2(jnp.maximum(jnp.abs(value), 1e-30)))


def solve(gram, count):
    g = lambda m, n: gram[(min(m, n), max(m, n))]
    scale = jnp.sqrt(g(1, 1) + epsilon)
    combos = {1: {1: 1.0 / scale}}
    hess = {(1, 0): scale}
    for j in range(1, count):
        d = {j + 1: None}
        for m in range(1, j + 1):
            d[m] = 0.0
        for i in range(1, j + 1):
            h = 0.0
            for m, c in combos[i].items():
                h = h + c * g(m, j + 1)
            hess[(i, j)] = h
            for m, c in combos[i].items():
                d[m] = d[m] - h * c
        square = g(j + 1, j + 1)
        for m in range(1, j + 1):
            inner = 2.0 * g(m, j + 1)
            for n in range(1, j + 1):
                inner = inner + d[n] * g(m, n)
            square = square + d[m] * inner
        length = jnp.sqrt(jnp.maximum(square, 1e-7 * g(j + 1, j + 1)) + epsilon)
        hess[(j + 1, j)] = length
        inv = 1.0 / length
        combos[j + 1] = {m: (inv if m == j + 1 else d[m] * inv) for m in d}
    return combos, hess


def call(kernel, outs, *operands, scratch=(), far=(), limit=16):
    vmem = pl.BlockSpec(memory_space=pltpu.VMEM)
    specs = [
        pl.BlockSpec(memory_space=pltpu.SMEM) if a.dtype == jnp.int32 else vmem for a in operands
    ]
    for i in far:
        specs[i] = pl.BlockSpec(memory_space=pl.ANY)
    return pl.pallas_call(
        kernel,
        out_shape=outs,
        in_specs=specs,
        out_specs=jax.tree.map(lambda _: vmem, outs),
        scratch_shapes=scratch,
        compiler_params=pltpu.CompilerParams(vmem_limit_bytes=limit << 20),
    )(*operands)


def extras(n_fields):
    return (1 + 3 * n_fields + 7) // 8 * 8


def matmul_kernel(n_fields, exact, at_ref, kept_ref, got_ref, w_ref, *refs):
    own_refs, other_refs = refs[:n_fields], refs[n_fields : 2 * n_fields]
    out_ref, x_ref = refs[2 * n_fields :][:2]
    core, place, side = at_ref[0], at_ref[1], at_ref[2]
    cells = w_ref.shape[1]
    copies = []
    if exact:
        held_ref, sems = refs[-2:]
        for h in range(2):
            copies.append(
                pltpu.make_async_copy(kept_ref.at[:, h, 0], held_ref.at[:, h], sems.at[h])
            )
            copies[h].start()

    for ref, k in ((own_refs[-1], core), (other_refs[-1], 1 - core)):
        for i in range(NX):
            t, o = divmod(i, 2)
            x, half = (place + 2 * NZ - 2 * k - t) % NX, (k + o + side) % 2
            value = ref[t, o]
            rows = pl.ds(pl.multiple_of(half * HALF + x * SUB, SUB), SUB)
            high = value.astype(jnp.bfloat16)
            x_ref[rows, pl.ds(0, cells)] = high
            if not exact:
                low = (value - high.astype(jnp.float32)).astype(jnp.bfloat16)
                x_ref[rows, pl.ds(cells, cells)] = low
    for g in (2, 3, 0, 1):
        y = (g + 2 * core) % NY
        total = None
        if exact and g < 2:
            copies[g].wait()
        for j in range(TERMS):
            if g >= 2:
                rates = got_ref[j, g - 2]
            else:
                rates = held_ref[j, g] if exact else kept_ref[j, g, 0]
            product = jnp.dot(rates, x_ref[...], preferred_element_type=jnp.float32)
            if not exact:
                product = product[:, :cells] + product[:, cells:]
            product = w_ref[pl.ds(j, 1), :] * product
            total = product if total is None else total + product
        for x in range(NX):
            block = total[x * SUB : (x + 1) * SUB, :]
            if exact:
                out_ref[x, y] = block
                continue
            power = exponent(jnp.max(jnp.abs(block), axis=0, keepdims=True))
            out_ref[x, y, pl.ds(0, SUB), :] = block * jnp.exp2(-power)
            out_ref[x, y, pl.ds(SUB, 1), :] = power
    if not exact:
        extra_ref = refs[-1]
        extra_ref[...] = jnp.zeros_like(extra_ref)
        for m in range(n_fields):
            total = jnp.zeros((8, cells), jnp.float32)
            for a_ref, b_ref in ((own_refs[m], own_refs[-1]), (other_refs[m], other_refs[-1])):
                product = a_ref[...] * b_ref[...]
                total = total + jnp.sum(product.reshape(HALF // 8, 8, cells), axis=0)
            total = jnp.sum(total, axis=0, keepdims=True)
            power = exponent(total)
            total = total * jnp.exp2(-power)
            high = total.astype(jnp.bfloat16).astype(jnp.float32)
            extra_ref[pl.ds(3 * m + 1, 1), :] = power
            extra_ref[pl.ds(3 * m + 2, 1), :] = high
            extra_ref[pl.ds(3 * m + 3, 1), :] = (total - high) * 256.0
        for b in range(NX * NY):
            x, y = divmod(b, NY)
            out_ref[x, y, pl.ds(SUB + 1, extra_ref.shape[0] - 1), :] = extra_ref[pl.ds(1, extra_ref.shape[0] - 1), :]


def apply_rates(at, kept, got, weights, fields, exact):
    cells = weights.shape[1]
    more = 0 if exact else extras(len(fields))
    rows = SUB + more
    own, other = [f[0] for f in fields], [f[1] for f in fields]
    if exact:
        held = pltpu.VMEM((TERMS, 2, HALF, COLS), kept.dtype)
        last = [held, pltpu.SemaphoreType.DMA((2,))]
    else:
        last = [pltpu.VMEM((more, cells), jnp.float32)]

    def kernel(*refs):
        matmul_kernel(len(fields), exact, *refs)

    out = call(
        kernel,
        jax.ShapeDtypeStruct((NX, NY, rows, cells), jnp.float32),
        at,
        kept,
        got,
        weights,
        *own,
        *other,
        scratch=[pltpu.VMEM((COLS, cells if exact else 2 * cells), jnp.bfloat16)] + last,
        far=(1,) if exact else (),
        limit=46 if exact else 16,
    )
    return out.reshape(NX * NY, rows, cells)


def combine_kernel(j, got_ref, gram_ref, *refs):
    q_refs, outs = refs[:j], refs[j:]
    fresh, inner = None, [None] * j
    for b in range(NX * NY):
        value = got_ref[b, pl.ds(0, SUB), :]
        if j > 0:
            extra = got_ref[b, pl.ds(SUB, extras(j)), :]
            value = value * jnp.exp2(extra[:1])
        fresh = value if fresh is None else fresh + value
        for m in range(j):
            value = extra[3 * m + 2 : 3 * m + 3] + extra[3 * m + 3 : 3 * m + 4] * (1.0 / 256.0)
            value = value * jnp.exp2(extra[3 * m + 1 : 3 * m + 2])
            inner[m] = value if inner[m] is None else inner[m] + value
    gram_out = outs[-1]
    gram = {}
    if j > 0:
        gram_out[...] = gram_ref[...]
        for m in range(1, j + 1):
            for n in range(m, j):
                gram[(m, n)] = gram_ref[pl.ds(4 * (m - 1) + n - 1, 1), :]
            row = inner[m - 1]
            gram[(m, j)] = row
            gram_out[pl.ds(4 * (m - 1) + j - 1, 1), :] = row
        _, hess = solve(gram, j)
        for i in range(1, j):
            fresh = fresh - hess[(i, j - 1)] * q_refs[i][...]
        fresh = fresh * (1.0 / hess[(j, j - 1)])
    else:
        gram_out[...] = jnp.zeros_like(gram_out)
    if j < KRYLOV:
        outs[0][...] = fresh
    else:
        dots = outs[0]
        lanes = dots.shape[1]
        for m in range(1, KRYLOV + 1):
            row = jnp.sum(q_refs[m - 1][...] * fresh, axis=0, keepdims=True)
            dots[pl.ds(m - 1, 1), :] = row[:, :lanes]
            dots[pl.ds(KRYLOV + m - 1, 1), :] = row[:, lanes:]


def combine(j, got, gram, fields):
    cells = got.shape[2]

    def kernel(*refs):
        combine_kernel(j, *refs)

    if j < KRYLOV:
        outs = (jax.ShapeDtypeStruct((SUB, cells), jnp.float32),)
    else:
        outs = (jax.ShapeDtypeStruct((2 * KRYLOV, cells // 2), jnp.float32),)
    outs = (*outs, jax.ShapeDtypeStruct(gram.shape, jnp.float32))
    return call(kernel, outs, got, gram, *fields)


def pair_kernel(mine_ref, other_ref, out_ref):
    out_ref[...] = jnp.broadcast_to((mine_ref[...] + other_ref[...])[None], out_ref.shape)


def finish_kernel(p_ref, q_ref, gram_ref, dots_ref, out_ref):
    gram = {}
    for m in range(1, KRYLOV + 1):
        for n in range(m, KRYLOV + 1):
            gram[(m, n)] = gram_ref[pl.ds(4 * (m - 1) + n - 1, 1), :]
    dots = jnp.sum(dots_ref[...], axis=0)
    last = {
        m: jnp.concatenate([dots[m - 1 : m], dots[KRYLOV + m - 1 : KRYLOV + m]], axis=1)
        for m in range(1, KRYLOV + 1)
    }
    combos, hess = solve(gram, KRYLOV)
    for i in range(1, KRYLOV + 1):
        h = 0.0
        for m, c in combos[i].items():
            h = h + c * last[m]
        hess[(i, KRYLOV)] = h
    zero = jnp.zeros_like(gram[(1, 1)])
    unit = [zero + 1.0] + [zero] * (KRYLOV - 1)
    coeffs = [u / float(math.factorial(TAYLOR + 1)) for u in unit]
    for k in range(TAYLOR - 1, -1, -1):
        fresh = []
        for i in range(1, KRYLOV + 1):
            value = unit[i - 1] / float(math.factorial(k + 1))
            for j in range(max(i - 1, 1), KRYLOV + 1):
                value = value + step_size * hess[(i, j)] * coeffs[j - 1]
            fresh.append(value)
        coeffs = fresh
    out = p_ref[...]
    for m in range(1, KRYLOV + 1):
        factor = 0.0
        for i in range(m, KRYLOV + 1):
            factor = factor + coeffs[i - 1] * combos[i][m]
        out = out + step_size * hess[(1, 0)] * factor * q_ref[m - 1]
    out_ref[...] = out


def body(rate_terms, populations, temp_bins, bin_coeffs):
    core = lax.axis_index("k")
    n_bins = bin_coeffs.shape[0]
    cells = populations.shape[1]
    exchange = lambda v, axes: lax.all_to_all(v, axes, 0, 0, tiled=True)

    halves = rate_terms.reshape(TERMS, 2, NK, HALF, COLS)
    away = halves[:, :, 1]
    kept = pltpu.with_memory_space_constraint(halves, pltpu.VMEM)

    onehot = (temp_bins[:, None] == jnp.arange(n_bins, dtype=jnp.int32)[None, :]).astype(
        jnp.float32
    )
    weights = jnp.dot(onehot, bin_coeffs, precision=lax.Precision.HIGHEST)
    weights = jnp.pad(weights.T, ((0, 2), (0, 0)))
    at = jnp.stack([core, lax.axis_index("z"), lax.axis_index("y") // 2]).astype(jnp.int32)

    def spread(both):
        wide = jnp.float32 if both.dtype == WIRE else both.dtype
        own = [lax.ppermute(both, ("z", "k", "x"), pairs) for pairs in SPREAD]
        own = jnp.stack(own)
        other = lax.ppermute(own, "k", SWAP)
        return own.astype(wide), other.astype(wide)

    def reduce(partial):
        return exchange(partial.astype(WIRE), ("x", "y")).astype(jnp.float32)

    piece = lax.ppermute(populations.astype(jnp.bfloat16), ALL, TO_INNER)
    both = jnp.stack([piece, lax.ppermute(piece, "k", SWAP)])
    away, both = lax.optimization_barrier((away, both))
    got = lax.ppermute(away, "k", SWAP)
    got = pltpu.with_memory_space_constraint(got, pltpu.VMEM)
    first = spread(both)
    met = reduce(apply_rates(at, halves, got, weights, [first], True))
    gram = jnp.zeros((16, cells), jnp.float32)
    q, gram = combine(0, met, gram, [])
    pieces, fields = [q], []
    for j in range(1, KRYLOV + 1):
        piece = q.astype(WIRE)
        both = jnp.stack([piece, lax.ppermute(piece, "k", SWAP)])
        fields.append(spread(both))
        if j == KRYLOV:
            inner = jnp.stack(pieces).astype(WIRE)
        partial = apply_rates(at, kept, got, weights, fields, False)
        met = reduce(partial)
        if j < KRYLOV:
            q, gram = combine(j, met, gram, pieces)
            pieces.append(q)
        else:
            dots, gram = combine(j, met, gram, pieces)
            inner, dots = lax.optimization_barrier((inner, dots))
            outer = lax.ppermute(inner, ALL, TO_OUTER)
    dots = call(
        pair_kernel,
        jax.ShapeDtypeStruct((NZ * NX * NY, *dots.shape), dots.dtype),
        dots,
        lax.ppermute(dots, "k", SWAP),
    )
    dots = exchange(dots, ("z", "x", "y"))
    outer = outer.astype(jnp.float32)
    out = jax.ShapeDtypeStruct(populations.shape, jnp.float32)
    return call(finish_kernel, out, populations, outer, gram, dots)


def solution(mesh):
    named = Mesh(mesh.devices.reshape(NZ, NK, NX, NY), ALL)
    placed = (P(None, ("z", "k"), ("x", "y")), P(ALL, None), P(), P())
    return jax.shard_map(body, mesh=named, in_specs=placed, out_specs=P(ALL, None), check_vma=False)
```

```python
import math

import jax
import jax.numpy as jnp
from jax import lax
from jax.experimental import pallas as pl
from jax.experimental.pallas import tpu as pltpu
from jax.sharding import Mesh, PartitionSpec as P


KRYLOV = 4
TAYLOR = 8
TERMS = 6

epsilon = 1e-06
step_size = 1.0

NZ, NK, NX, NY = 4, 2, 4, 4
ALL = ("z", "k", "x", "y")
SUB = 64
HALF = NX * SUB
COLS = NK * HALF
WIRE = jnp.float16


def device(z, k, x, y):
    return ((z * NK + k) * NX + x) * NY + y


TO_INNER = [
    (device(z, k, x, y), device(z, (k + x) % 2, y, 2 * k + x // 2))
    for z in range(NZ)
    for k in range(NK)
    for x in range(NX)
    for y in range(NY)
]
TO_OUTER = [(b, a) for a, b in TO_INNER]
SWAP = [(0, 1), (1, 0)]
SPREAD = [
    [
        ((z * NK + k) * NX + x, (((x + k + 2 - 2 * t) % NZ) * NK + k) * NX + z)
        for z in range(NZ)
        for k in range(NK)
        for x in range(NX)
    ]
    for t in range(2)
]


def exponent(value):
    return jnp.floor(jnp.log2(jnp.maximum(jnp.abs(value), 1e-30)))


def solve(gram, count):
    g = lambda m, n: gram[(min(m, n), max(m, n))]
    scale = jnp.sqrt(g(1, 1) + epsilon)
    combos = {1: {1: 1.0 / scale}}
    hess = {(1, 0): scale}
    for j in range(1, count):
        d = {j + 1: None}
        for m in range(1, j + 1):
            d[m] = 0.0
        for i in range(1, j + 1):
            h = 0.0
            for m, c in combos[i].items():
                h = h + c * g(m, j + 1)
            hess[(i, j)] = h
            for m, c in combos[i].items():
                d[m] = d[m] - h * c
        square = g(j + 1, j + 1)
        for m in range(1, j + 1):
            inner = 2.0 * g(m, j + 1)
            for n in range(1, j + 1):
                inner = inner + d[n] * g(m, n)
            square = square + d[m] * inner
        length = jnp.sqrt(jnp.maximum(square, 1e-7 * g(j + 1, j + 1)) + epsilon)
        hess[(j + 1, j)] = length
        inv = 1.0 / length
        combos[j + 1] = {m: (inv if m == j + 1 else d[m] * inv) for m in d}
    return combos, hess


def call(kernel, outs, *operands, scratch=(), far=(), limit=16):
    vmem = pl.BlockSpec(memory_space=pltpu.VMEM)
    specs = [
        pl.BlockSpec(memory_space=pltpu.SMEM) if a.dtype == jnp.int32 else vmem for a in operands
    ]
    for i in far:
        specs[i] = pl.BlockSpec(memory_space=pl.ANY)
    return pl.pallas_call(
        kernel,
        out_shape=outs,
        in_specs=specs,
        out_specs=jax.tree.map(lambda _: vmem, outs),
        scratch_shapes=scratch,
        compiler_params=pltpu.CompilerParams(vmem_limit_bytes=limit << 20),
    )(*operands)


def extras(n_fields):
    return (1 + 3 * n_fields + 7) // 8 * 8


def matmul_kernel(n_fields, exact, at_ref, kept_ref, got_ref, w_ref, *refs):
    own_refs, other_refs = refs[:n_fields], refs[n_fields : 2 * n_fields]
    out_ref, x_ref = refs[2 * n_fields :][:2]
    core, place, side = at_ref[0], at_ref[1], at_ref[2]
    cells = w_ref.shape[1]
    copies = []
    if exact:
        held_ref, sems = refs[-2:]
        for h in range(2):
            copies.append(
                pltpu.make_async_copy(kept_ref.at[:, h, 0], held_ref.at[:, h], sems.at[h])
            )
            copies[h].start()

    for ref, k in ((own_refs[-1], core), (other_refs[-1], 1 - core)):
        for i in range(NX):
            t, o = divmod(i, 2)
            x, half = (place + 2 * NZ - k - 2 + 2 * t) % NX, (k + o + side) % 2
            value = ref[t, o]
            rows = pl.ds(pl.multiple_of(half * HALF + x * SUB, SUB), SUB)
            high = value.astype(jnp.bfloat16)
            x_ref[rows, pl.ds(0, cells)] = high
            if not exact:
                low = (value - high.astype(jnp.float32)).astype(jnp.bfloat16)
                x_ref[rows, pl.ds(cells, cells)] = low
    for g in (2, 3, 0, 1):
        y = (g + 2 * core) % NY
        total = None
        if exact and g < 2:
            copies[g].wait()
        for j in range(TERMS):
            if g >= 2:
                rates = got_ref[j, g - 2]
            else:
                rates = held_ref[j, g] if exact else kept_ref[j, g, 0]
            product = jnp.dot(rates, x_ref[...], preferred_element_type=jnp.float32)
            if not exact:
                product = product[:, :cells] + product[:, cells:]
            product = w_ref[pl.ds(j, 1), :] * product
            total = product if total is None else total + product
        for x in range(NX):
            block = total[x * SUB : (x + 1) * SUB, :]
            if exact:
                out_ref[x, y] = block
                continue
            power = exponent(jnp.max(jnp.abs(block), axis=0, keepdims=True))
            out_ref[x, y, pl.ds(0, SUB), :] = block * jnp.exp2(-power)
            out_ref[x, y, pl.ds(SUB, 1), :] = power
    if not exact:
        extra_ref = refs[-1]
        extra_ref[...] = jnp.zeros_like(extra_ref)
        for m in range(n_fields):
            total = jnp.zeros((8, cells), jnp.float32)
            for a_ref, b_ref in ((own_refs[m], own_refs[-1]), (other_refs[m], other_refs[-1])):
                product = a_ref[...] * b_ref[...]
                total = total + jnp.sum(product.reshape(HALF // 8, 8, cells), axis=0)
            total = jnp.sum(total, axis=0, keepdims=True)
            power = exponent(total)
            total = total * jnp.exp2(-power)
            high = total.astype(jnp.bfloat16).astype(jnp.float32)
            extra_ref[pl.ds(3 * m + 1, 1), :] = power
            extra_ref[pl.ds(3 * m + 2, 1), :] = high
            extra_ref[pl.ds(3 * m + 3, 1), :] = (total - high) * 256.0
        for b in range(NX * NY):
            x, y = divmod(b, NY)
            out_ref[x, y, pl.ds(SUB + 1, extra_ref.shape[0] - 1), :] = extra_ref[pl.ds(1, extra_ref.shape[0] - 1), :]


def apply_rates(at, kept, got, weights, fields, exact):
    cells = weights.shape[1]
    more = 0 if exact else extras(len(fields))
    rows = SUB + more
    own, other = [f[0] for f in fields], [f[1] for f in fields]
    if exact:
        held = pltpu.VMEM((TERMS, 2, HALF, COLS), kept.dtype)
        last = [held, pltpu.SemaphoreType.DMA((2,))]
    else:
        last = [pltpu.VMEM((more, cells), jnp.float32)]

    def kernel(*refs):
        matmul_kernel(len(fields), exact, *refs)

    out = call(
        kernel,
        jax.ShapeDtypeStruct((NX, NY, rows, cells), jnp.float32),
        at,
        kept,
        got,
        weights,
        *own,
        *other,
        scratch=[pltpu.VMEM((COLS, cells if exact else 2 * cells), jnp.bfloat16)] + last,
        far=(1,) if exact else (),
        limit=46 if exact else 16,
    )
    return out.reshape(NX * NY, rows, cells)


def combine_kernel(j, got_ref, gram_ref, *refs):
    q_refs, outs = refs[:j], refs[j:]
    fresh, inner = None, [None] * j
    for b in range(NX * NY):
        value = got_ref[b, pl.ds(0, SUB), :]
        if j > 0:
            extra = got_ref[b, pl.ds(SUB, extras(j)), :]
            value = value * jnp.exp2(extra[:1])
        fresh = value if fresh is None else fresh + value
        for m in range(j):
            value = extra[3 * m + 2 : 3 * m + 3] + extra[3 * m + 3 : 3 * m + 4] * (1.0 / 256.0)
            value = value * jnp.exp2(extra[3 * m + 1 : 3 * m + 2])
            inner[m] = value if inner[m] is None else inner[m] + value
    gram_out = outs[-1]
    gram = {}
    if j > 0:
        gram_out[...] = gram_ref[...]
        for m in range(1, j + 1):
            for n in range(m, j):
                gram[(m, n)] = gram_ref[pl.ds(4 * (m - 1) + n - 1, 1), :]
            row = inner[m - 1]
            gram[(m, j)] = row
            gram_out[pl.ds(4 * (m - 1) + j - 1, 1), :] = row
        _, hess = solve(gram, j)
        for i in range(1, j):
            fresh = fresh - hess[(i, j - 1)] * q_refs[i][...]
        fresh = fresh * (1.0 / hess[(j, j - 1)])
    else:
        gram_out[...] = jnp.zeros_like(gram_out)
    if j < KRYLOV:
        outs[0][...] = fresh
    else:
        dots = outs[0]
        lanes = dots.shape[1]
        for m in range(1, KRYLOV + 1):
            row = jnp.sum(q_refs[m - 1][...] * fresh, axis=0, keepdims=True)
            dots[pl.ds(m - 1, 1), :] = row[:, :lanes]
            dots[pl.ds(KRYLOV + m - 1, 1), :] = row[:, lanes:]


def combine(j, got, gram, fields):
    cells = got.shape[2]

    def kernel(*refs):
        combine_kernel(j, *refs)

    if j < KRYLOV:
        outs = (jax.ShapeDtypeStruct((SUB, cells), jnp.float32),)
    else:
        outs = (jax.ShapeDtypeStruct((2 * KRYLOV, cells // 2), jnp.float32),)
    outs = (*outs, jax.ShapeDtypeStruct(gram.shape, jnp.float32))
    return call(kernel, outs, got, gram, *fields)


def pair_kernel(mine_ref, other_ref, out_ref):
    out_ref[...] = jnp.broadcast_to((mine_ref[...] + other_ref[...])[None], out_ref.shape)


def finish_kernel(p_ref, q_ref, gram_ref, dots_ref, out_ref):
    gram = {}
    for m in range(1, KRYLOV + 1):
        for n in range(m, KRYLOV + 1):
            gram[(m, n)] = gram_ref[pl.ds(4 * (m - 1) + n - 1, 1), :]
    dots = jnp.sum(dots_ref[...], axis=0)
    last = {
        m: jnp.concatenate([dots[m - 1 : m], dots[KRYLOV + m - 1 : KRYLOV + m]], axis=1)
        for m in range(1, KRYLOV + 1)
    }
    combos, hess = solve(gram, KRYLOV)
    for i in range(1, KRYLOV + 1):
        h = 0.0
        for m, c in combos[i].items():
            h = h + c * last[m]
        hess[(i, KRYLOV)] = h
    zero = jnp.zeros_like(gram[(1, 1)])
    unit = [zero + 1.0] + [zero] * (KRYLOV - 1)
    coeffs = [u / float(math.factorial(TAYLOR + 1)) for u in unit]
    for k in range(TAYLOR - 1, -1, -1):
        fresh = []
        for i in range(1, KRYLOV + 1):
            value = unit[i - 1] / float(math.factorial(k + 1))
            for j in range(max(i - 1, 1), KRYLOV + 1):
                value = value + step_size * hess[(i, j)] * coeffs[j - 1]
            fresh.append(value)
        coeffs = fresh
    out = p_ref[...]
    for m in range(1, KRYLOV + 1):
        factor = 0.0
        for i in range(m, KRYLOV + 1):
            factor = factor + coeffs[i - 1] * combos[i][m]
        out = out + step_size * hess[(1, 0)] * factor * q_ref[m - 1]
    out_ref[...] = out


def body(rate_terms, populations, temp_bins, bin_coeffs):
    core = lax.axis_index("k")
    n_bins = bin_coeffs.shape[0]
    cells = populations.shape[1]
    exchange = lambda v, axes: lax.all_to_all(v, axes, 0, 0, tiled=True)

    halves = rate_terms.reshape(TERMS, 2, NK, HALF, COLS)
    away = halves[:, :, 1]
    kept = pltpu.with_memory_space_constraint(halves, pltpu.VMEM)

    onehot = (temp_bins[:, None] == jnp.arange(n_bins, dtype=jnp.int32)[None, :]).astype(
        jnp.float32
    )
    weights = jnp.dot(onehot, bin_coeffs, precision=lax.Precision.HIGHEST)
    weights = jnp.pad(weights.T, ((0, 2), (0, 0)))
    at = jnp.stack([core, lax.axis_index("z"), lax.axis_index("y") // 2]).astype(jnp.int32)

    def spread(both):
        wide = jnp.float32 if both.dtype == WIRE else both.dtype
        own = [lax.ppermute(both, ("z", "k", "x"), pairs) for pairs in SPREAD]
        own = jnp.stack(own)
        other = lax.ppermute(own, "k", SWAP)
        return own.astype(wide), other.astype(wide)

    def reduce(partial):
        return exchange(partial.astype(WIRE), ("x", "y")).astype(jnp.float32)

    piece = lax.ppermute(populations.astype(jnp.bfloat16), ALL, TO_INNER)
    both = jnp.stack([piece, lax.ppermute(piece, "k", SWAP)])
    away, both = lax.optimization_barrier((away, both))
    got = lax.ppermute(away, "k", SWAP)
    got = pltpu.with_memory_space_constraint(got, pltpu.VMEM)
    first = spread(both)
    met = reduce(apply_rates(at, halves, got, weights, [first], True))
    gram = jnp.zeros((16, cells), jnp.float32)
    q, gram = combine(0, met, gram, [])
    pieces, fields = [q], []
    for j in range(1, KRYLOV + 1):
        piece = q.astype(WIRE)
        both = jnp.stack([piece, lax.ppermute(piece, "k", SWAP)])
        fields.append(spread(both))
        if j == KRYLOV:
            inner = jnp.stack(pieces).astype(WIRE)
            fields[-1], inner = lax.optimization_barrier((fields[-1], inner))
        partial = apply_rates(at, kept, got, weights, fields, False)
        met = reduce(partial)
        if j < KRYLOV:
            q, gram = combine(j, met, gram, pieces)
            pieces.append(q)
        else:
            dots, gram = combine(j, met, gram, pieces)
            inner, dots = lax.optimization_barrier((inner, dots))
            outer = lax.ppermute(inner, ALL, TO_OUTER)
    dots = call(
        pair_kernel,
        jax.ShapeDtypeStruct((NZ * NX * NY, *dots.shape), dots.dtype),
        dots,
        lax.ppermute(dots, "k", SWAP),
    )
    dots = exchange(dots, ("z", "x", "y"))
    outer = outer.astype(jnp.float32)
    out = jax.ShapeDtypeStruct(populations.shape, jnp.float32)
    return call(finish_kernel, out, populations, outer, gram, dots)


def solution(mesh):
    named = Mesh(mesh.devices.reshape(NZ, NK, NX, NY), ALL)
    placed = (P(None, ("z", "k"), ("x", "y")), P(ALL, None), P(), P())
    return jax.shard_map(body, mesh=named, in_specs=placed, out_specs=P(ALL, None), check_vma=False)
```

```python
import math

import jax
import jax.numpy as jnp
from jax import lax
from jax.experimental import pallas as pl
from jax.experimental.pallas import tpu as pltpu
from jax.sharding import Mesh, PartitionSpec as P


KRYLOV = 4
TAYLOR = 8
TERMS = 6

epsilon = 1e-06
step_size = 1.0

NZ, NK, NX, NY = 4, 2, 4, 4
ALL = ("z", "k", "x", "y")
SUB = 64
HALF = NX * SUB
COLS = NK * HALF
WIRE = jnp.float16


def device(z, k, x, y):
    return ((z * NK + k) * NX + x) * NY + y


TO_INNER = [
    (device(z, k, x, y), device(z, (k + x) % 2, y, 2 * k + x // 2))
    for z in range(NZ)
    for k in range(NK)
    for x in range(NX)
    for y in range(NY)
]
TO_OUTER = [(b, a) for a, b in TO_INNER]
SWAP = [(0, 1), (1, 0)]
SPREAD = [
    [
        ((z * NK + k) * NX + x, (((x + k + 2 * t) % NZ) * NK + k) * NX + z)
        for z in range(NZ)
        for k in range(NK)
        for x in range(NX)
    ]
    for t in range(2)
]


def exponent(value):
    return jnp.floor(jnp.log2(jnp.maximum(jnp.abs(value), 1e-30)))


def solve(gram, count):
    g = lambda m, n: gram[(min(m, n), max(m, n))]
    scale = jnp.sqrt(g(1, 1) + epsilon)
    combos = {1: {1: 1.0 / scale}}
    hess = {(1, 0): scale}
    for j in range(1, count):
        d = {j + 1: None}
        for m in range(1, j + 1):
            d[m] = 0.0
        for i in range(1, j + 1):
            h = 0.0
            for m, c in combos[i].items():
                h = h + c * g(m, j + 1)
            hess[(i, j)] = h
            for m, c in combos[i].items():
                d[m] = d[m] - h * c
        square = g(j + 1, j + 1)
        for m in range(1, j + 1):
            inner = 2.0 * g(m, j + 1)
            for n in range(1, j + 1):
                inner = inner + d[n] * g(m, n)
            square = square + d[m] * inner
        length = jnp.sqrt(jnp.maximum(square, 1e-7 * g(j + 1, j + 1)) + epsilon)
        hess[(j + 1, j)] = length
        inv = 1.0 / length
        combos[j + 1] = {m: (inv if m == j + 1 else d[m] * inv) for m in d}
    return combos, hess


def call(kernel, outs, *operands, scratch=(), far=(), limit=16):
    vmem = pl.BlockSpec(memory_space=pltpu.VMEM)
    specs = [
        pl.BlockSpec(memory_space=pltpu.SMEM) if a.dtype == jnp.int32 else vmem for a in operands
    ]
    for i in far:
        specs[i] = pl.BlockSpec(memory_space=pl.ANY)
    return pl.pallas_call(
        kernel,
        out_shape=outs,
        in_specs=specs,
        out_specs=jax.tree.map(lambda _: vmem, outs),
        scratch_shapes=scratch,
        compiler_params=pltpu.CompilerParams(vmem_limit_bytes=limit << 20),
    )(*operands)


def extras(n_fields):
    return (1 + 3 * n_fields + 7) // 8 * 8


def matmul_kernel(n_fields, exact, at_ref, kept_ref, got_ref, w_ref, *refs):
    own_refs, other_refs = refs[:n_fields], refs[n_fields : 2 * n_fields]
    out_ref, x_ref = refs[2 * n_fields :][:2]
    core, place, side = at_ref[0], at_ref[1], at_ref[2]
    cells = w_ref.shape[1]
    copies = []
    if exact:
        held_ref, sems = refs[-2:]
        for h in range(2):
            copies.append(
                pltpu.make_async_copy(kept_ref.at[:, h, 0], held_ref.at[:, h], sems.at[h])
            )
            copies[h].start()

    for ref, k in ((own_refs[-1], core), (other_refs[-1], 1 - core)):
        for i in range(NX):
            t, o = divmod(i, 2)
            x, half = (place + 2 * NZ - k - 2 * t) % NX, (k + o + side) % 2
            value = ref[t, o]
            rows = pl.ds(pl.multiple_of(half * HALF + x * SUB, SUB), SUB)
            high = value.astype(jnp.bfloat16)
            x_ref[rows, pl.ds(0, cells)] = high
            if not exact:
                low = (value - high.astype(jnp.float32)).astype(jnp.bfloat16)
                x_ref[rows, pl.ds(cells, cells)] = low
    for g in (2, 3, 0, 1):
        y = (g + 2 * core) % NY
        total = None
        if exact and g < 2:
            copies[g].wait()
        for j in range(TERMS):
            if g >= 2:
                rates = got_ref[j, g - 2]
            else:
                rates = held_ref[j, g] if exact else kept_ref[j, g, 0]
            product = jnp.dot(rates, x_ref[...], preferred_element_type=jnp.float32)
            if not exact:
                product = product[:, :cells] + product[:, cells:]
            product = w_ref[pl.ds(j, 1), :] * product
            total = product if total is None else total + product
        for x in range(NX):
            block = total[x * SUB : (x + 1) * SUB, :]
            if exact:
                out_ref[y, x] = block
                continue
            power = exponent(jnp.max(jnp.abs(block), axis=0, keepdims=True))
            out_ref[y, x, pl.ds(0, SUB), :] = block * jnp.exp2(-power)
            out_ref[y, x, pl.ds(SUB, 1), :] = power
    if not exact:
        extra_ref = refs[-1]
        extra_ref[...] = jnp.zeros_like(extra_ref)
        for m in range(n_fields):
            total = jnp.zeros((8, cells), jnp.float32)
            for a_ref, b_ref in ((own_refs[m], own_refs[-1]), (other_refs[m], other_refs[-1])):
                product = a_ref[...] * b_ref[...]
                total = total + jnp.sum(product.reshape(HALF // 8, 8, cells), axis=0)
            total = jnp.sum(total, axis=0, keepdims=True)
            power = exponent(total)
            total = total * jnp.exp2(-power)
            high = total.astype(jnp.bfloat16).astype(jnp.float32)
            extra_ref[pl.ds(3 * m + 1, 1), :] = power
            extra_ref[pl.ds(3 * m + 2, 1), :] = high
            extra_ref[pl.ds(3 * m + 3, 1), :] = (total - high) * 256.0
        for b in range(NX * NY):
            x, y = divmod(b, NY)
            out_ref[y, x, pl.ds(SUB + 1, extra_ref.shape[0] - 1), :] = extra_ref[pl.ds(1, extra_ref.shape[0] - 1), :]


def apply_rates(at, kept, got, weights, fields, exact):
    cells = weights.shape[1]
    more = 0 if exact else extras(len(fields))
    rows = SUB + more
    own, other = [f[0] for f in fields], [f[1] for f in fields]
    if exact:
        held = pltpu.VMEM((TERMS, 2, HALF, COLS), kept.dtype)
        last = [held, pltpu.SemaphoreType.DMA((2,))]
    else:
        last = [pltpu.VMEM((more, cells), jnp.float32)]

    def kernel(*refs):
        matmul_kernel(len(fields), exact, *refs)

    out = call(
        kernel,
        jax.ShapeDtypeStruct((NY, NX, rows, cells), jnp.float32),
        at,
        kept,
        got,
        weights,
        *own,
        *other,
        scratch=[pltpu.VMEM((COLS, cells if exact else 2 * cells), jnp.bfloat16)] + last,
        far=(1,) if exact else (),
        limit=46 if exact else 16,
    )
    return out.reshape(NX * NY, rows, cells)


def combine_kernel(j, got_ref, gram_ref, *refs):
    q_refs, outs = refs[:j], refs[j:]
    fresh, inner = None, [None] * j
    for b in range(NX * NY):
        value = got_ref[b, pl.ds(0, SUB), :]
        if j > 0:
            extra = got_ref[b, pl.ds(SUB, extras(j)), :]
            value = value * jnp.exp2(extra[:1])
        fresh = value if fresh is None else fresh + value
        for m in range(j):
            value = extra[3 * m + 2 : 3 * m + 3] + extra[3 * m + 3 : 3 * m + 4] * (1.0 / 256.0)
            value = value * jnp.exp2(extra[3 * m + 1 : 3 * m + 2])
            inner[m] = value if inner[m] is None else inner[m] + value
    gram_out = outs[-1]
    gram = {}
    if j > 0:
        gram_out[...] = gram_ref[...]
        for m in range(1, j + 1):
            for n in range(m, j):
                gram[(m, n)] = gram_ref[pl.ds(4 * (m - 1) + n - 1, 1), :]
            row = inner[m - 1]
            gram[(m, j)] = row
            gram_out[pl.ds(4 * (m - 1) + j - 1, 1), :] = row
        _, hess = solve(gram, j)
        for i in range(1, j):
            fresh = fresh - hess[(i, j - 1)] * q_refs[i][...]
        fresh = fresh * (1.0 / hess[(j, j - 1)])
    else:
        gram_out[...] = jnp.zeros_like(gram_out)
    if j < KRYLOV:
        outs[0][...] = fresh
    else:
        dots = outs[0]
        lanes = dots.shape[1]
        for m in range(1, KRYLOV + 1):
            row = jnp.sum(q_refs[m - 1][...] * fresh, axis=0, keepdims=True)
            dots[pl.ds(m - 1, 1), :] = row[:, :lanes]
            dots[pl.ds(KRYLOV + m - 1, 1), :] = row[:, lanes:]


def combine(j, got, gram, fields):
    cells = got.shape[2]

    def kernel(*refs):
        combine_kernel(j, *refs)

    if j < KRYLOV:
        outs = (jax.ShapeDtypeStruct((SUB, cells), jnp.float32),)
    else:
        outs = (jax.ShapeDtypeStruct((2 * KRYLOV, cells // 2), jnp.float32),)
    outs = (*outs, jax.ShapeDtypeStruct(gram.shape, jnp.float32))
    return call(kernel, outs, got, gram, *fields)


def pair_kernel(mine_ref, other_ref, out_ref):
    out_ref[...] = jnp.broadcast_to((mine_ref[...] + other_ref[...])[None], out_ref.shape)


def finish_kernel(p_ref, q_ref, gram_ref, dots_ref, out_ref):
    gram = {}
    for m in range(1, KRYLOV + 1):
        for n in range(m, KRYLOV + 1):
            gram[(m, n)] = gram_ref[pl.ds(4 * (m - 1) + n - 1, 1), :]
    dots = jnp.sum(dots_ref[...], axis=0)
    last = {
        m: jnp.concatenate([dots[m - 1 : m], dots[KRYLOV + m - 1 : KRYLOV + m]], axis=1)
        for m in range(1, KRYLOV + 1)
    }
    combos, hess = solve(gram, KRYLOV)
    for i in range(1, KRYLOV + 1):
        h = 0.0
        for m, c in combos[i].items():
            h = h + c * last[m]
        hess[(i, KRYLOV)] = h
    zero = jnp.zeros_like(gram[(1, 1)])
    unit = [zero + 1.0] + [zero] * (KRYLOV - 1)
    coeffs = [u / float(math.factorial(TAYLOR + 1)) for u in unit]
    for k in range(TAYLOR - 1, -1, -1):
        fresh = []
        for i in range(1, KRYLOV + 1):
            value = unit[i - 1] / float(math.factorial(k + 1))
            for j in range(max(i - 1, 1), KRYLOV + 1):
                value = value + step_size * hess[(i, j)] * coeffs[j - 1]
            fresh.append(value)
        coeffs = fresh
    out = p_ref[...]
    for m in range(1, KRYLOV + 1):
        factor = 0.0
        for i in range(m, KRYLOV + 1):
            factor = factor + coeffs[i - 1] * combos[i][m]
        out = out + step_size * hess[(1, 0)] * factor * q_ref[m - 1]
    out_ref[...] = out


def body(rate_terms, populations, temp_bins, bin_coeffs):
    core = lax.axis_index("k")
    n_bins = bin_coeffs.shape[0]
    cells = populations.shape[1]
    exchange = lambda v, axes: lax.all_to_all(v, axes, 0, 0, tiled=True)

    halves = rate_terms.reshape(TERMS, 2, NK, HALF, COLS)
    away = halves[:, :, 1]
    kept = pltpu.with_memory_space_constraint(halves, pltpu.VMEM)

    onehot = (temp_bins[:, None] == jnp.arange(n_bins, dtype=jnp.int32)[None, :]).astype(
        jnp.float32
    )
    weights = jnp.dot(onehot, bin_coeffs, precision=lax.Precision.HIGHEST)
    weights = jnp.pad(weights.T, ((0, 2), (0, 0)))
    at = jnp.stack([core, lax.axis_index("z"), lax.axis_index("y") // 2]).astype(jnp.int32)

    def spread(both):
        wide = jnp.float32 if both.dtype == WIRE else both.dtype
        own = [lax.ppermute(both, ("z", "k", "x"), pairs) for pairs in SPREAD]
        own = jnp.stack(own)
        other = lax.ppermute(own, "k", SWAP)
        return own.astype(wide), other.astype(wide)

    def reduce(partial):
        return exchange(partial.astype(WIRE), ("y", "x")).astype(jnp.float32)

    piece = lax.ppermute(populations.astype(jnp.bfloat16), ALL, TO_INNER)
    both = jnp.stack([piece, lax.ppermute(piece, "k", SWAP)])
    away, both = lax.optimization_barrier((away, both))
    got = lax.ppermute(away, "k", SWAP)
    got = pltpu.with_memory_space_constraint(got, pltpu.VMEM)
    first = spread(both)
    met = reduce(apply_rates(at, halves, got, weights, [first], True))
    gram = jnp.zeros((16, cells), jnp.float32)
    q, gram = combine(0, met, gram, [])
    pieces, fields = [q], []
    for j in range(1, KRYLOV + 1):
        piece = q.astype(WIRE)
        both = jnp.stack([piece, lax.ppermute(piece, "k", SWAP)])
        fields.append(spread(both))
        if j == KRYLOV:
            inner = jnp.stack(pieces).astype(WIRE)
            fields[-1], inner = lax.optimization_barrier((fields[-1], inner))
        partial = apply_rates(at, kept, got, weights, fields, False)
        met = reduce(partial)
        if j < KRYLOV:
            q, gram = combine(j, met, gram, pieces)
            pieces.append(q)
        else:
            dots, gram = combine(j, met, gram, pieces)
            inner, dots = lax.optimization_barrier((inner, dots))
            outer = lax.ppermute(inner, ALL, TO_OUTER)
    dots = call(
        pair_kernel,
        jax.ShapeDtypeStruct((NZ * NX * NY, *dots.shape), dots.dtype),
        dots,
        lax.ppermute(dots, "k", SWAP),
    )
    dots = exchange(dots, ("z", "x", "y"))
    outer = outer.astype(jnp.float32)
    out = jax.ShapeDtypeStruct(populations.shape, jnp.float32)
    return call(finish_kernel, out, populations, outer, gram, dots)


def solution(mesh):
    named = Mesh(mesh.devices.reshape(NZ, NK, NX, NY), ALL)
    placed = (P(None, ("z", "k"), ("x", "y")), P(ALL, None), P(), P())
    return jax.shard_map(body, mesh=named, in_specs=placed, out_specs=P(ALL, None), check_vma=False)
```
